256 devices in a mesh: tm: 64 (over x, z, core), space: 4 (over y).
Axes of the slice: x: 4, y: 4, z: 8, core: 2. Of those that a mesh axis runs over, the one named last changes fastest.
Arguments:
- snapshots: float32 [4096, 16384], P('tm', 'space'), as said below
- space_factor: float32 [16384, 256], P('space'), as said below
Outputs:
- time_factor: float32 [4096, 256], P('tm')
- loadings: float32 [256, 16384], P('tm', 'space')
Inputs may be any that keep to these rules, and one draw needn't show every extreme that they name: `snapshots`: entries are real values. `space_factor`: entries are real values; columns have norms between 0.05 and 1, the previous sweep's singular values.
All inputs are finite; a program needn't handle non-finite values.
Results may differ from the reference program's by a relative error of at most 0.0001.
Values sent between devices are 32-bit elements; how exact they have to be, the bound alone decides.
A program may use at most 64 MiB of HBM per device.

```python
import math
import jax
import jax.numpy as jnp
from jax import lax

P_SIZE = 16384
RANK = 256
NS = 2
TIME = 4096


def draw_snapshots(key, part):
    keys = jax.random.split(jax.random.fold_in(key, 11), 3)
    ramp = jnp.arange(TIME, dtype=jnp.float32) / TIME
    row_scale = jnp.exp(ramp * math.log(3.0)) * jnp.exp(jax.random.uniform(keys[1], (TIME,)) * math.log(10.0)) / 6.0
    base = jax.random.normal(keys[0], (TIME, P_SIZE), jnp.float32)
    col_scale = jnp.exp(jax.random.uniform(keys[2], (P_SIZE,)) * math.log(10.0)) / 3.2
    return base * row_scale[:, None] * col_scale[None, :]


def draw_space_factor(key, part):
    keys = jax.random.split(jax.random.fold_in(key, 23), 2)
    base = jax.random.normal(keys[0], (P_SIZE, RANK), jnp.float32)
    col_scale = jnp.exp(jax.random.uniform(keys[1], (RANK,)) * math.log(10.0)) / 10.0
    return base * col_scale[None, :] / math.sqrt(P_SIZE)


def setup_inputs(seed: int = 0) -> dict:
    key_of = jax.random.split(jax.random.key(seed), 3)
    snapshots = draw_snapshots(jax.random.fold_in(key_of[2], 71), 0)
    space_factor = draw_space_factor(jax.random.fold_in(key_of[2], 71), 0)
    return dict(snapshots=snapshots, space_factor=space_factor)


def reference(snapshots, space_factor):
    highest = lax.Precision.HIGHEST
    projected = jnp.dot(snapshots, space_factor, precision=highest, preferred_element_type=jnp.float32)
    factor = projected / jnp.sqrt(jnp.sum(projected * projected))
    identity_mat = jnp.eye(RANK, dtype=jnp.float32)
    for sweep in range(NS):
        correlation = jnp.dot(factor.T, factor, precision=highest, preferred_element_type=jnp.float32)
        factor = jnp.dot(factor, 1.5 * identity_mat - 0.5 * correlation, precision=highest, preferred_element_type=jnp.float32)
    loadings = jnp.dot(factor.T, snapshots, precision=highest, preferred_element_type=jnp.float32)
    return (factor * jnp.float32(math.sqrt(TIME)), loadings)
```

```python
import math

import jax
import jax.numpy as jnp
from jax import lax
from jax.experimental import pallas as pl
from jax.experimental.pallas import tpu as pltpu
from jax.sharding import PartitionSpec as P

MESH = pl.DeviceIdType.MESH
F32, BF16 = jnp.float32, jnp.bfloat16
RANK = 256
TIME = 4096
NX, NY, NZ = 4, 4, 8
ROWS = 64
COLS = 4096
WIDE = COLS // NX
CHUNK = WIDE // NZ
HALF = RANK // 2
LOADS = 8
EARLY = 3


def split(value):
    high = value.astype(BF16)
    return high, (value - high.astype(F32)).astype(BF16)


def dot(left, right, dims=((1,), (0,))):
    return lax.dot_general(left, right, (dims, ((), ())), preferred_element_type=F32)


def dot3(left, right, dims=((1,), (0,))):
    return dot(left[0], right[0], dims) + (dot(left[0], right[1], dims) + dot(left[1], right[0], dims))


def kernel(
    snap_hbm, space_hbm, time_out, load_out,
    xv, sv, part, pair, from_y, yg, yt, xg, gram, gram_x, gram_z, corr, fth, ftl,
    lp, lp_peer, up, up_in, down, down_in, full, mixed, land,
    ld_x, ld_s, xs, xr, ys, yr, ags, agr, gxs, gxr, gzs, gzr, cs, cr, ps, pr,
    us, ur, ds, dr, fs, fr, ms, mr,
):
    t, y = lax.axis_index("tm"), lax.axis_index("space")
    x, z, c = t // 16, (t // 2) % NZ, t % 2
    other = 1 - c

    def dev(x_, y_, z_, c_):
        return {"tm": x_ * 16 + z_ * 2 + c_, "space": y_}

    def remote(src, dst, send, recv, to):
        return pltpu.make_async_remote_copy(
            src_ref=src, dst_ref=dst, send_sem=send, recv_sem=recv, device_id=to, device_id_type=MESH
        )

    partner = dev(x, y, z, other)
    flip_a = dev(x, y + 1 - 2 * (y % 2), z, c)
    flip_b = dev(x, NY - 1 - y, z, c)

    load_x = pltpu.make_async_copy(snap_hbm, xv, ld_x)
    load_x.start()
    depth = COLS // LOADS
    load_s = [
        pltpu.make_async_copy(space_hbm.at[pl.ds(i * depth, depth)], sv.at[pl.ds(i * depth, depth)], ld_s.at[i])
        for i in range(LOADS)
    ]
    for copy in load_s:
        copy.start()

    barrier = pltpu.get_barrier_semaphore()
    greeted = [flip_a, flip_b, partner]
    greeted += [dev((x + i) % NX, y, z, k) for i in range(1, NX) for k in range(2)]
    greeted += [dev(x, y, (z + i) % NZ, c) for i in range(1, NZ)]
    for to in greeted:
        pl.semaphore_signal(barrier, inc=1, device_id=to, device_id_type=MESH)

    load_x.wait()
    acc = jnp.zeros((ROWS, RANK), F32)
    acc2 = jnp.zeros((2 * ROWS, RANK), F32)
    for i in range(LOADS):
        load_s[i].wait()
        xh, xl = split(xv[:, i * depth:(i + 1) * depth])
        sh, sl = split(sv[i * depth:(i + 1) * depth, :])
        acc2 = acc2 + dot(jnp.concatenate([xh, xl], axis=0), sh)
        acc = acc + dot(xh, sl)
    part[...] = acc2[:ROWS] + (acc2[ROWS:] + acc)
    pl.semaphore_wait(barrier, len(greeted))

    top, low = pl.ds(0, ROWS // 2), pl.ds(ROWS // 2, ROWS // 2)
    first = [
        remote(part.at[top], from_y.at[0], ys.at[0], yr.at[0], flip_a),
        remote(part.at[low], from_y.at[1], ys.at[1], yr.at[1], flip_b),
    ]
    for copy in first:
        copy.start()

    order = [(z + 4) % NZ, (z + 5) % NZ, (z + 3) % NZ, (z + 6) % NZ, (z + 2) % NZ, (z + 7) % NZ, (z + 1) % NZ, z]

    def send_columns(slots):
        for s in slots:
            for i in (2, 1, 3):
                xp = (x + i) % NX
                at = pl.multiple_of(xp * WIDE + order[s] * CHUNK, CHUNK)
                remote(xv.at[:, pl.ds(at, CHUNK)], xg.at[order[s], x], xs, xr.at[s], dev(xp, y, z, c)).start()

    send_columns(range(EARLY))
    for d in range(NZ):
        xg[d, x] = xv[:, pl.ds(pl.multiple_of(x * WIDE + d * CHUNK, CHUNK), CHUNK)]

    first[0].wait_recv()
    pair[:ROWS // 2] = part[:ROWS // 2] + from_y[0]
    second = [remote(pair.at[top], from_y.at[2], ys.at[2], yr.at[2], flip_b)]
    second[0].start()
    first[1].wait_recv()
    pair[ROWS // 2:] = part[ROWS // 2:] + from_y[1]
    second.append(remote(pair.at[low], from_y.at[3], ys.at[3], yr.at[3], flip_a))
    second[1].start()
    second[0].wait_recv()
    second[1].wait_recv()
    mine = jnp.concatenate([pair[:ROWS // 2] + from_y[2], pair[ROWS // 2:] + from_y[3]], axis=0)
    yg[x] = mine

    parts = split(mine)
    share = dot3(parts, parts, ((0,), (0,)))
    energy = jnp.sum(jnp.sum(mine * mine, axis=0, keepdims=True), axis=1, keepdims=True)
    energy = jnp.broadcast_to(energy, (8, 128))
    for b in range(NY):
        for k in range(8):
            gram[b, k, :, :RANK] = share[64 * b + 8 * k:64 * b + 8 * k + 8]
            gram[b, k, :, RANK:] = energy
    me8 = 2 * x + c
    gram_x[me8] = gram[y, me8]
    for i in (2, 1, 3, 0):
        for k in range(2):
            if i == 0 and k == 0:
                continue
            xp, cp = (x + i) % NX, (c + k) % 2
            remote(gram.at[y, 2 * xp + cp], gram_x.at[me8], gxs, gxr, dev(xp, y, z, cp)).start()

    for i in (2, 1, 3):
        remote(yg.at[x], yg.at[x], ags, agr, dev((x + i) % NX, y, z, c)).start()
    send_columns(range(EARLY, NZ))

    remote(gram_x.at[pl.ds(0, 7)], gram_x.at[pl.ds(0, 7)], gxs, gxr, partner).wait_recv()
    total = gram_x[0]
    for k in range(1, 8):
        total = total + gram_x[k]
    gram_z[z] = total
    for i in (4, 3, 5, 2, 6, 1, 7):
        remote(gram_z.at[z], gram_z.at[z], gzs, gzr, dev(x, y, (z + i) % NZ, c)).start()

    remote(yg.at[pl.ds(0, 3)], yg.at[pl.ds(0, 3)], ags, agr, partner).wait_recv()
    for i in range(NX):
        yt[:, i * ROWS:(i + 1) * ROWS] = yg[i].T

    remote(gram_z.at[pl.ds(0, 7)], gram_z.at[pl.ds(0, 7)], gzs, gzr, partner).wait_recv()
    total = gram_z[0]
    for k in range(1, NZ):
        total = total + gram_z[k]
    block = 8 * y + me8
    corr[block] = total[:, :RANK]
    scale = 1.0 / jnp.sqrt(total[0:1, RANK:RANK + 1])
    for i in (2, 1, 3, 0):
        for j in (2, 1, 3, 0):
            for k in range(2):
                if i == 0 and j == 0 and k == 0:
                    continue
                to = dev((x + i) % NX, (y + j) % NY, z, (c + k) % 2)
                remote(corr.at[block], corr.at[block], cs, cr, to).start()

    fth[...], ftl[...] = split(yt[...] * scale)
    swaps = [None] * NZ

    def form(s):
        d = order[s]
        remote(xg.at[d, pl.ds(0, 3)], xg.at[d, pl.ds(0, 3)], xs, xr.at[s], partner).wait_recv()
        cols = split(xg[d].reshape(NX * ROWS, CHUNK))
        value = dot3((fth[...], ftl[...]), cols)
        lp[d, 0] = value[:HALF]
        lp[d, 1] = value[HALF:]
        swaps[s] = remote(lp.at[d, other], lp_peer.at[d], ps.at[s], pr.at[s], partner)
        swaps[s].start()

    def held(s):
        swaps[s].wait_recv()
        return lp[order[s], c] + lp_peer[order[s]]

    above, below = dev(x, y, (z + 1) % NZ, c), dev(x, y, (z + 7) % NZ, c)
    ups = [remote(up.at[s], up_in.at[s], us.at[s], ur.at[s], above) for s in range(4)]
    downs = [remote(down.at[s], down_in.at[s], ds.at[s], dr.at[s], below) for s in range(3)]

    for s in range(4):
        form(s)
    up[0] = held(0)
    ups[0].start()
    down[0] = held(1)
    downs[0].start()
    form(4)
    form(5)
    for s in range(1, 3):
        value = held(2 * s)
        ups[s - 1].wait_recv()
        up[s] = value + up_in[s - 1]
        ups[s].start()
        value = held(2 * s + 1)
        downs[s - 1].wait_recv()
        down[s] = value + down_in[s - 1]
        downs[s].start()
        if s == 1:
            form(6)
            form(7)

    remote(corr.at[pl.ds(0, 31)], corr.at[pl.ds(0, 31)], cs, cr, partner).wait_recv()
    a1 = corr[...].reshape(RANK, RANK) * scale * scale
    a1s = split(a1)
    a2 = dot3(a1s, a1s)
    a4 = dot3(split(a2), split(a2 - 9.0 * a1))
    row = lax.broadcasted_iota(jnp.int32, (RANK, RANK), 0)
    col = lax.broadcasted_iota(jnp.int32, (RANK, RANK), 1)
    poly = jnp.where(row == col, 2.25, 0.0) + (a4 + (27.0 * a2 - 39.0 * a1)) * 0.0625
    polys = split(poly)

    value = held(6)
    ups[2].wait_recv()
    up[3] = value + up_in[2]
    ups[3].start()
    time_out[...] = dot3(split(yg[x] * scale), polys) * math.sqrt(TIME)
    value = held(7)
    downs[2].wait_recv()
    value = value + down_in[2]
    ups[3].wait_recv()
    full[c] = value + up_in[3]
    share_full = remote(full.at[c], full.at[c], fs, fr, partner)
    share_full.start()
    share_full.wait_recv()

    value = dot3(polys, split(full[...].reshape(RANK, CHUNK)))
    value = jnp.where(c == 0, value, pltpu.roll(value, RANK - 4, 0))
    for k in range(NX * NZ):
        mixed[k] = value[8 * k:8 * k + 4]
    spot = NZ * x + z
    land[spot] = mixed[spot]
    for i in (2, 1, 3, 0):
        for j in (4, 3, 5, 2, 6, 1, 7, 0):
            if i == 0 and j == 0:
                continue
            xp, zp = (x + i) % NX, (z + j) % NZ
            remote(mixed.at[NZ * xp + zp], land.at[spot], ms, mr, dev(xp, y, zp, c)).start()
    remote(land.at[pl.ds(0, 31)], land.at[pl.ds(0, 31)], ms, mr, partner).wait_recv()
    for k in range(NX * NZ):
        load_out[:, k * CHUNK:(k + 1) * CHUNK] = land[k]

    for copy in first + second + swaps + ups + downs + [share_full]:
        copy.wait_send()
    remote(xg.at[pl.ds(0, 6)], xg.at[pl.ds(0, 6)], xs, xr.at[0], partner).wait_send()
    remote(yg.at[pl.ds(0, 3)], yg.at[pl.ds(0, 3)], ags, agr, partner).wait_send()
    remote(gram_x.at[pl.ds(0, 7)], gram_x.at[pl.ds(0, 7)], gxs, gxr, partner).wait_send()
    remote(gram_z.at[pl.ds(0, 7)], gram_z.at[pl.ds(0, 7)], gzs, gzr, partner).wait_send()
    remote(corr.at[pl.ds(0, 31)], corr.at[pl.ds(0, 31)], cs, cr, partner).wait_send()
    remote(land.at[pl.ds(0, 31)], land.at[pl.ds(0, 31)], ms, mr, partner).wait_send()


def on_device(snapshots, space_factor):
    vm, dma = pltpu.VMEM, pltpu.SemaphoreType.DMA
    return pl.pallas_call(
        kernel,
        name="hooi_time",
        out_shape=(jax.ShapeDtypeStruct((ROWS, RANK), F32), jax.ShapeDtypeStruct((RANK // 64, COLS), F32)),
        in_specs=[pl.BlockSpec(memory_space=pl.ANY)] * 2,
        out_specs=(pl.BlockSpec(memory_space=pltpu.VMEM),) * 2,
        scratch_shapes=[
            vm((ROWS, COLS), F32), vm((COLS, RANK), F32),
            vm((ROWS, RANK), F32), vm((ROWS, RANK), F32), vm((4, ROWS // 2, RANK), F32),
            vm((NX, ROWS, RANK), F32), vm((RANK, NX * ROWS), F32),
            vm((NZ, NX, ROWS, CHUNK), F32),
            vm((NY, 8, 8, RANK + 128), F32), vm((8, 8, RANK + 128), F32), vm((NZ, 8, RANK + 128), F32),
            vm((32, 8, RANK), F32),
            vm((RANK, RANK), BF16), vm((RANK, RANK), BF16),
            vm((NZ, 2, HALF, CHUNK), F32), vm((NZ, HALF, CHUNK), F32),
            vm((4, HALF, CHUNK), F32), vm((4, HALF, CHUNK), F32),
            vm((3, HALF, CHUNK), F32), vm((3, HALF, CHUNK), F32),
            vm((2, HALF, CHUNK), F32),
            vm((32, 4, CHUNK), F32), vm((32, 4, CHUNK), F32),
            dma, dma((LOADS,)), dma, dma((NZ,)), dma((4,)), dma((4,)), dma, dma, dma, dma, dma, dma, dma, dma,
            dma((NZ,)), dma((NZ,)), dma((4,)), dma((4,)), dma((3,)), dma((3,)), dma, dma, dma, dma,
        ],
        compiler_params=pltpu.CompilerParams(collective_id=0, has_side_effects=True),
    )(snapshots, space_factor)


def solution(mesh):
    return jax.shard_map(
        on_device,
        mesh=mesh,
        in_specs=(P("tm", "space"), P("space", None)),
        out_specs=(P("tm", None), P("tm", "space")),
        check_vma=False,
    )
```

```python
import math

import jax
import jax.numpy as jnp
from jax import lax
from jax.experimental import pallas as pl
from jax.experimental.pallas import tpu as pltpu
from jax.sharding import PartitionSpec as P

MESH = pl.DeviceIdType.MESH
F32, BF16 = jnp.float32, jnp.bfloat16
RANK = 256
TIME = 4096
NX, NY, NZ = 4, 4, 8
ROWS = 64
COLS = 4096
WIDE = COLS // NX
CHUNK = WIDE // NZ
HALF = RANK // 2
LOADS = 4
EARLY = 2
SUBS = 2
SUB = HALF // SUBS


def split(value):
    high = value.astype(BF16)
    return high, (value - high.astype(F32)).astype(BF16)


def dot(left, right, dims=((1,), (0,))):
    return lax.dot_general(left, right, (dims, ((), ())), preferred_element_type=F32)


def dot3(left, right, dims=((1,), (0,))):
    return dot(left[0], right[0], dims) + (dot(left[0], right[1], dims) + dot(left[1], right[0], dims))


def kernel(
    snap_hbm, space_hbm, time_out, load_out,
    xv, sv, py, yg, yt, xc, xg, gram, gram_x, gram_z, corr, fth, ftl, polh, poll,
    lp, lp_peer, up, up_in, down, down_in, full, mixed, land, peak_x, peak_y, peak_z,
    ld_x, ld_s, xs, xr, ys, yr, ags, agr, gxs, gxr, gzs, gzr, cs, cr, ps, pr,
    us, ur, ds, dr, fs, fr, ms, mr, pxs, pxr, pys, pyr, pzs, pzr, near,
):
    t, y = lax.axis_index("tm"), lax.axis_index("space")
    x, z, c = t // 16, (t // 2) % NZ, t % 2
    other = 1 - c

    def dev(x_, y_, z_, c_):
        return {"tm": x_ * 16 + z_ * 2 + c_, "space": y_}

    def remote(src, dst, send, recv, to):
        return pltpu.make_async_remote_copy(
            src_ref=src, dst_ref=dst, send_sem=send, recv_sem=recv, device_id=to, device_id_type=MESH
        )

    partner = dev(x, y, z, other)
    above, below = dev(x, y, (z + 1) % NZ, c), dev(x, y, (z + 7) % NZ, c)
    me8 = 2 * x + c

    def peak_of(value):
        value = jnp.max(jnp.max(value, axis=0, keepdims=True), axis=1, keepdims=True)
        return jnp.broadcast_to(value, (1, 128))

    def peak_among(ref):
        value = ref[0]
        for k in range(1, ref.shape[0]):
            value = jnp.maximum(value, ref[k])
        return value

    load_x = pltpu.make_async_copy(snap_hbm, xv, ld_x)
    load_x.start()
    depth = COLS // LOADS
    load_s = [
        pltpu.make_async_copy(space_hbm.at[pl.ds(i * depth, depth)], sv.at[pl.ds(i * depth, depth)], ld_s.at[i])
        for i in range(LOADS)
    ]
    for copy in load_s:
        copy.start()

    barrier = pltpu.get_barrier_semaphore()
    greeted = [partner, above, below] + [dev(x, (y + i) % NY, z, c) for i in (2, 1, 3)]
    greeted += [dev((x + i) % NX, y, z, k) for i in (2, 1, 3) for k in range(2)]
    for to in greeted:
        pl.semaphore_signal(barrier, inc=1, device_id=to, device_id_type=MESH)

    load_x.wait()
    acc = jnp.zeros((ROWS, RANK), F32)
    acc2 = jnp.zeros((2 * ROWS, RANK), F32)
    for i in range(LOADS):
        load_s[i].wait()
        xh, xl = split(xv[:, i * depth:(i + 1) * depth])
        sh, sl = split(sv[i * depth:(i + 1) * depth, :])
        acc2 = acc2 + dot(jnp.concatenate([xh, xl], axis=0), sh)
        acc = acc + dot(xh, sl)
    py[y] = acc2[:ROWS] + (acc2[ROWS:] + acc)
    pl.semaphore_wait(barrier, len(greeted))

    for i in (2, 1, 3):
        remote(py.at[y], py.at[y], ys, yr, dev(x, (y + i) % NY, z, c)).start()

    def pass_on(step):
        for to in (above, below):
            pl.semaphore_signal(near.at[step], inc=1, device_id=to, device_id_type=MESH)

    pass_on(0)
    peak_x[me8] = peak_of(jnp.abs(py[y]))
    for i in (2, 1, 3, 0):
        for k in range(2):
            if i or k:
                remote(peak_x.at[me8], peak_x.at[me8], pxs, pxr, dev((x + i) % NX, y, z, (c + k) % 2)).start()

    order = [(z + 4) % NZ, (z + 5) % NZ, (z + 3) % NZ, (z + 6) % NZ, (z + 2) % NZ, (z + 7) % NZ, (z + 1) % NZ, z]
    for s in range(NZ):
        for i in range(NX):
            xc[i, s] = xv[:, pl.ds(pl.multiple_of(i * WIDE + order[s] * CHUNK, CHUNK), CHUNK)]

    def send_columns(p):
        slots = pl.ds(2 * p, 2)
        for i in (2, 1, 3):
            xp = (x + i) % NX
            remote(xc.at[xp, slots], xg.at[x, slots], xs.at[p], xr.at[p], dev(xp, y, z, c)).start()

    def got_columns(p):
        some = xg.at[pl.ds(0, 3), pl.ds(2 * p, 2)]
        return remote(some, some, xs.at[p], xr.at[p], partner)

    for p in range(EARLY):
        send_columns(p)
    xg[x] = xc[x]
    pl.semaphore_wait(near.at[0], 2)
    pass_on(1)
    remote(peak_x.at[pl.ds(0, 7)], peak_x.at[pl.ds(0, 7)], pxs, pxr, partner).wait_recv()
    peak_y[y] = peak_among(peak_x)
    for i in (2, 1, 3):
        remote(peak_y.at[y], peak_y.at[y], pys, pyr, dev(x, (y + i) % NY, z, c)).start()
    pl.semaphore_wait(near.at[1], 2)
    pass_on(2)
    remote(py.at[pl.ds(0, 3)], py.at[pl.ds(0, 3)], ys, yr, partner).wait_recv()
    mine = (py[0] + py[1]) + (py[2] + py[3])

    yg[x] = mine
    for i in (2, 1, 3):
        remote(yg.at[x], yg.at[x], ags, agr, dev((x + i) % NX, y, z, c)).start()

    high, low_part = split(mine)
    share = dot(
        jnp.concatenate([high, high, low_part], axis=0), jnp.concatenate([high, low_part, high], axis=0), ((0,), (0,))
    )
    for b in range(NY):
        for k in range(8):
            gram[b, k] = share[64 * b + 8 * k:64 * b + 8 * k + 8]
    gram_x[me8] = gram[y, me8]
    for i in (2, 1, 3, 0):
        for k in range(2):
            if i or k:
                xp, cp = (x + i) % NX, (c + k) % 2
                remote(gram.at[y, 2 * xp + cp], gram_x.at[me8], gxs, gxr, dev(xp, y, z, cp)).start()
    for p in range(EARLY, NZ // 2):
        send_columns(p)

    remote(peak_y.at[pl.ds(0, 3)], peak_y.at[pl.ds(0, 3)], pys, pyr, partner).wait_recv()
    peak_z[z] = peak_among(peak_y)
    pl.semaphore_wait(near.at[2], 2)
    for i in (4, 3, 5, 2, 6, 1, 7):
        remote(peak_z.at[z], peak_z.at[z], pzs, pzr, dev(x, y, (z + i) % NZ, c)).start()

    remote(yg.at[pl.ds(0, 3)], yg.at[pl.ds(0, 3)], ags, agr, partner).wait_recv()
    for i in range(NX):
        yt[:, i * ROWS:(i + 1) * ROWS] = yg[i].T
    remote(peak_z.at[pl.ds(0, 7)], peak_z.at[pl.ds(0, 7)], pzs, pzr, partner).wait_recv()
    peak = peak_among(peak_z)[:, :1] * 1024.0

    fth[...], ftl[...] = split(yt[...] * (1.0 / peak))
    swaps = [None] * NZ

    def form(p):
        slots = (2 * p, 2 * p + 1)
        got_columns(p).wait_recv()
        cols = split(jnp.concatenate([xg[:, s].reshape(NX * ROWS, CHUNK) for s in slots], axis=1))
        value = dot3((fth[...], ftl[...]), cols)
        for i, s in enumerate(slots):
            for h in range(2):
                lp[s, h] = value[h * HALF:(h + 1) * HALF, i * CHUNK:(i + 1) * CHUNK]
            swaps[s] = remote(lp.at[s, other], lp_peer.at[s], ps.at[s], pr.at[s], partner)
            swaps[s].start()

    def held(s):
        swaps[s].wait_recv()
        return (lp[s, c] + lp_peer[s]).reshape(SUBS, SUB, CHUNK)

    ups = [[remote(up.at[s, q], up_in.at[s, q], us.at[s, q], ur.at[s, q], above) for q in range(SUBS)] for s in range(4)]
    downs = [
        [remote(down.at[s, q], down_in.at[s, q], ds.at[s, q], dr.at[s, q], below) for q in range(SUBS)] for s in range(3)
    ]

    def hop(s):
        ahead = held(2 * s)
        back = held(2 * s + 1) if s < 3 else None
        for q in range(SUBS):
            value = ahead[q]
            if s:
                ups[s - 1][q].wait_recv()
                value = value + up_in[s - 1, q]
            up[s, q] = value
            ups[s][q].start()
            if s == 3:
                continue
            value = back[q]
            if s:
                downs[s - 1][q].wait_recv()
                value = value + down_in[s - 1, q]
            down[s, q] = value
            downs[s][q].start()

    form(0)
    form(1)
    hop(0)

    remote(gram_x.at[pl.ds(0, 7)], gram_x.at[pl.ds(0, 7)], gxs, gxr, partner).wait_recv()
    total = gram_x[0]
    for k in range(1, 8):
        total = total + gram_x[k]
    gram_z[z] = total
    for i in (4, 3, 5, 2, 6, 1, 7):
        remote(gram_z.at[z], gram_z.at[z], gzs, gzr, dev(x, y, (z + i) % NZ, c)).start()

    form(2)
    hop(1)

    remote(gram_z.at[pl.ds(0, 7)], gram_z.at[pl.ds(0, 7)], gzs, gzr, partner).wait_recv()
    total = gram_z[0]
    for k in range(1, NZ):
        total = total + gram_z[k]
    block = 8 * y + me8
    corr[block] = total
    for i in (2, 1, 3, 0):
        for j in (2, 1, 3, 0):
            for k in range(2):
                if i or j or k:
                    to = dev((x + i) % NX, (y + j) % NY, z, (c + k) % 2)
                    remote(corr.at[block], corr.at[block], cs, cr, to).start()

    form(3)
    hop(2)
    hop(3)

    remote(corr.at[pl.ds(0, 31)], corr.at[pl.ds(0, 31)], cs, cr, partner).wait_recv()
    row = lax.broadcasted_iota(jnp.int32, (RANK, RANK), 0)
    col = lax.broadcasted_iota(jnp.int32, (RANK, RANK), 1)
    whole = corr[...].reshape(RANK, RANK)
    energy = jnp.sum(jnp.sum(jnp.where(row == col, whole, 0.0), axis=0, keepdims=True), axis=1, keepdims=True)
    scale = 1.0 / jnp.sqrt(energy)
    a1 = whole * scale * scale
    a1s = split(a1)
    a2 = dot3(a1s, a1s)
    a4 = dot3(split(a2), split(a2 - 9.0 * a1))
    poly = jnp.where(row == col, 2.25, 0.0) + (a4 + (27.0 * a2 - 39.0 * a1)) * 0.0625
    high, low_part = split(poly)
    for h in range(2):
        polh[h] = high[:, h * HALF:(h + 1) * HALF]
        poll[h] = low_part[:, h * HALF:(h + 1) * HALF]

    last = held(NZ - 1)
    for q in range(SUBS):
        downs[2][q].wait_recv()
        ups[3][q].wait_recv()
        full[c, q * SUB:(q + 1) * SUB] = (last[q] + down_in[2, q] + up_in[3, q]) * (peak * scale)
    share_full = remote(full.at[c], full.at[c], fs, fr, partner)
    share_full.start()
    value = dot3((polh[c], poll[c]), split(full[c]))
    share_full.wait_recv()
    value = value + dot3((polh[other], poll[other]), split(full[other]))
    value = jnp.where(c == 0, value, pltpu.roll(value, RANK - 4, 0))
    for k in range(NX * NZ):
        mixed[k] = value[8 * k:8 * k + 4]
    spot = NZ * x + z
    land[spot] = mixed[spot]
    for i in (2, 1, 3, 0):
        for j in (4, 3, 5, 2, 6, 1, 7, 0):
            if i or j:
                xp, zp = (x + i) % NX, (z + j) % NZ
                remote(mixed.at[NZ * xp + zp], land.at[spot], ms, mr, dev(xp, y, zp, c)).start()
    time_out[...] = dot3(split(yg[x] * scale), (high, low_part)) * math.sqrt(TIME)
    remote(land.at[pl.ds(0, 31)], land.at[pl.ds(0, 31)], ms, mr, partner).wait_recv()
    for k in range(NX * NZ):
        load_out[:, k * CHUNK:(k + 1) * CHUNK] = land[k]

    for copy in swaps + sum(ups + downs, []) + [share_full] + [got_columns(p) for p in range(NZ // 2)]:
        copy.wait_send()
    remote(py.at[pl.ds(0, 3)], py.at[pl.ds(0, 3)], ys, yr, partner).wait_send()
    remote(yg.at[pl.ds(0, 3)], yg.at[pl.ds(0, 3)], ags, agr, partner).wait_send()
    remote(gram_x.at[pl.ds(0, 7)], gram_x.at[pl.ds(0, 7)], gxs, gxr, partner).wait_send()
    remote(gram_z.at[pl.ds(0, 7)], gram_z.at[pl.ds(0, 7)], gzs, gzr, partner).wait_send()
    remote(corr.at[pl.ds(0, 31)], corr.at[pl.ds(0, 31)], cs, cr, partner).wait_send()
    remote(land.at[pl.ds(0, 31)], land.at[pl.ds(0, 31)], ms, mr, partner).wait_send()
    remote(peak_x.at[pl.ds(0, 7)], peak_x.at[pl.ds(0, 7)], pxs, pxr, partner).wait_send()
    remote(peak_y.at[pl.ds(0, 3)], peak_y.at[pl.ds(0, 3)], pys, pyr, partner).wait_send()
    remote(peak_z.at[pl.ds(0, 7)], peak_z.at[pl.ds(0, 7)], pzs, pzr, partner).wait_send()


def on_device(snapshots, space_factor):
    vm, dma = pltpu.VMEM, pltpu.SemaphoreType.DMA
    return pl.pallas_call(
        kernel,
        name="hooi_time",
        out_shape=(jax.ShapeDtypeStruct((ROWS, RANK), F32), jax.ShapeDtypeStruct((RANK // 64, COLS), F32)),
        in_specs=[pl.BlockSpec(memory_space=pl.ANY)] * 2,
        out_specs=(pl.BlockSpec(memory_space=pltpu.VMEM),) * 2,
        scratch_shapes=[
            vm((ROWS, COLS), F32), vm((COLS, RANK), F32), vm((NY, ROWS, RANK), F32),
            vm((NX, ROWS, RANK), F32), vm((RANK, NX * ROWS), F32),
            vm((NX, NZ, ROWS, CHUNK), F32), vm((NX, NZ, ROWS, CHUNK), F32),
            vm((NY, 8, 8, RANK), F32), vm((8, 8, RANK), F32), vm((NZ, 8, RANK), F32),
            vm((32, 8, RANK), F32),
            vm((RANK, RANK), BF16), vm((RANK, RANK), BF16),
            vm((2, RANK, HALF), BF16), vm((2, RANK, HALF), BF16),
            vm((NZ, 2, HALF, CHUNK), F32), vm((NZ, HALF, CHUNK), F32),
            vm((4, SUBS, SUB, CHUNK), F32), vm((4, SUBS, SUB, CHUNK), F32),
            vm((3, SUBS, SUB, CHUNK), F32), vm((3, SUBS, SUB, CHUNK), F32),
            vm((2, HALF, CHUNK), F32),
            vm((32, 4, CHUNK), F32), vm((32, 4, CHUNK), F32),
            vm((8, 1, 128), F32), vm((NY, 1, 128), F32), vm((NZ, 1, 128), F32),
            dma, dma((LOADS,)), dma((4,)), dma((4,)), dma, dma, dma, dma, dma, dma, dma, dma, dma, dma,
            dma((NZ,)), dma((NZ,)), dma((4, SUBS)), dma((4, SUBS)), dma((3, SUBS)), dma((3, SUBS)), dma, dma, dma, dma,
            dma, dma, dma, dma, dma, dma, pltpu.SemaphoreType.REGULAR((3,)),
        ],
        compiler_params=pltpu.CompilerParams(collective_id=0, has_side_effects=True),
    )(snapshots, space_factor)


def solution(mesh):
    return jax.shard_map(
        on_device,
        mesh=mesh,
        in_specs=(P("tm", "space"), P("space", None)),
        out_specs=(P("tm", None), P("tm", "space")),
        check_vma=False,
    )
```

```python
import math

import jax
import jax.numpy as jnp
from jax import lax
from jax.experimental import pallas as pl
from jax.experimental.pallas import tpu as pltpu
from jax.sharding import PartitionSpec as P

MESH = pl.DeviceIdType.MESH
F32, BF16 = jnp.float32, jnp.bfloat16
RANK = 256
TIME = 4096
NX, NY, NZ = 4, 4, 8
ROWS = 64
COLS = 4096
WIDE = COLS // NX
CHUNK = WIDE // NZ
HALF = RANK // 2
LOADS = 4
EARLY = 2
SUBS = 2
SUB = HALF // SUBS


def split(value):
    high = value.astype(BF16)
    return high, (value - high.astype(F32)).astype(BF16)


def dot(left, right, dims=((1,), (0,))):
    return lax.dot_general(left, right, (dims, ((), ())), preferred_element_type=F32)


def dot3(left, right, dims=((1,), (0,))):
    return dot(left[0], right[0], dims) + (dot(left[0], right[1], dims) + dot(left[1], right[0], dims))


def kernel(
    snap_hbm, space_hbm, time_out, load_out,
    xv, sv, py, yg, yt, xc, xg, gram, gram_x, gram_z, corr, fth, ftl, polh, poll,
    lp, lp_peer, up, up_in, down, down_in, full, mixed, land, peak_x, peak_y, peak_z,
    ld_x, ld_s, xs, xr, ys, yr, ags, agr, gxs, gxr, gzs, gzr, cs, cr, ps, pr,
    us, ur, ds, dr, fs, fr, ms, mr, pxs, pxr, pys, pyr, pzs, pzr, near,
):
    t, y = lax.axis_index("tm"), lax.axis_index("space")
    x, z, c = t // 16, (t // 2) % NZ, t % 2
    other = 1 - c

    def dev(x_, y_, z_, c_):
        return {"tm": x_ * 16 + z_ * 2 + c_, "space": y_}

    def remote(src, dst, send, recv, to):
        return pltpu.make_async_remote_copy(
            src_ref=src, dst_ref=dst, send_sem=send, recv_sem=recv, device_id=to, device_id_type=MESH
        )

    partner = dev(x, y, z, other)
    above, below = dev(x, y, (z + 1) % NZ, c), dev(x, y, (z + 7) % NZ, c)
    me8 = 2 * x + c

    def peak_of(value):
        value = jnp.max(jnp.max(value, axis=0, keepdims=True), axis=1, keepdims=True)
        return jnp.broadcast_to(value, (1, 128))

    def peak_among(ref):
        value = ref[0]
        for k in range(1, ref.shape[0]):
            value = jnp.maximum(value, ref[k])
        return value

    load_x = pltpu.make_async_copy(snap_hbm, xv, ld_x)
    load_x.start()
    depth = COLS // LOADS
    load_s = [
        pltpu.make_async_copy(space_hbm.at[pl.ds(i * depth, depth)], sv.at[pl.ds(i * depth, depth)], ld_s.at[i])
        for i in range(LOADS)
    ]
    for copy in load_s:
        copy.start()

    barrier = pltpu.get_barrier_semaphore()
    greeted = [partner, above, below] + [dev(x, (y + i) % NY, z, c) for i in (2, 1, 3)]
    greeted += [dev((x + i) % NX, y, z, k) for i in (2, 1, 3) for k in range(2)]
    for to in greeted:
        pl.semaphore_signal(barrier, inc=1, device_id=to, device_id_type=MESH)

    load_x.wait()
    acc = jnp.zeros((ROWS, RANK), F32)
    acc2 = jnp.zeros((2 * ROWS, RANK), F32)
    for i in range(LOADS):
        load_s[i].wait()
        xh, xl = split(xv[:, i * depth:(i + 1) * depth])
        sh, sl = split(sv[i * depth:(i + 1) * depth, :])
        acc2 = acc2 + dot(jnp.concatenate([xh, xl], axis=0), sh)
        acc = acc + dot(xh, sl)
    py[y] = acc2[:ROWS] + (acc2[ROWS:] + acc)
    pl.semaphore_wait(barrier, len(greeted))

    for i in (2, 1, 3):
        remote(py.at[y], py.at[y], ys, yr, dev(x, (y + i) % NY, z, c)).start()

    def pass_on(step):
        for to in (above, below):
            pl.semaphore_signal(near.at[step], inc=1, device_id=to, device_id_type=MESH)

    pass_on(0)
    peak_x[me8] = peak_of(jnp.abs(py[y]))
    for i in (2, 1, 3, 0):
        for k in range(2):
            if i or k:
                remote(peak_x.at[me8], peak_x.at[me8], pxs, pxr, dev((x + i) % NX, y, z, (c + k) % 2)).start()

    order = [(z + 4) % NZ, (z + 5) % NZ, (z + 3) % NZ, (z + 6) % NZ, (z + 2) % NZ, (z + 7) % NZ, (z + 1) % NZ, z]
    for s in range(NZ):
        for i in range(NX):
            xc[i, s] = xv[:, pl.ds(pl.multiple_of(i * WIDE + order[s] * CHUNK, CHUNK), CHUNK)]

    def send_columns(p):
        slots = pl.ds(2 * p, 2)
        for i in (2, 1, 3):
            xp = (x + i) % NX
            remote(xc.at[xp, slots], xg.at[x, slots], xs.at[p], xr.at[p], dev(xp, y, z, c)).start()

    def got_columns(p):
        some = xg.at[pl.ds(0, 3), pl.ds(2 * p, 2)]
        return remote(some, some, xs.at[p], xr.at[p], partner)

    for p in range(EARLY):
        send_columns(p)
    xg[x] = xc[x]
    pl.semaphore_wait(near.at[0], 2)
    pass_on(1)
    remote(peak_x.at[pl.ds(0, 7)], peak_x.at[pl.ds(0, 7)], pxs, pxr, partner).wait_recv()
    peak_y[y] = peak_among(peak_x)
    for i in (2, 1, 3):
        remote(peak_y.at[y], peak_y.at[y], pys, pyr, dev(x, (y + i) % NY, z, c)).start()
    pl.semaphore_wait(near.at[1], 2)
    pass_on(2)
    remote(py.at[pl.ds(0, 3)], py.at[pl.ds(0, 3)], ys, yr, partner).wait_recv()
    mine = (py[0] + py[1]) + (py[2] + py[3])

    yg[x] = mine
    for i in (2, 1, 3):
        remote(yg.at[x], yg.at[x], ags, agr, dev((x + i) % NX, y, z, c)).start()

    remote(peak_y.at[pl.ds(0, 3)], peak_y.at[pl.ds(0, 3)], pys, pyr, partner).wait_recv()
    peak_z[z] = peak_among(peak_y)
    pl.semaphore_wait(near.at[2], 2)
    for i in (4, 3, 5, 2, 6, 1, 7):
        remote(peak_z.at[z], peak_z.at[z], pzs, pzr, dev(x, y, (z + i) % NZ, c)).start()

    left = split(yg[x, :, pl.ds(pl.multiple_of(y // 2 * HALF, HALF), HALF)])
    high, low_part = split(mine)
    share = dot(
        jnp.concatenate([left[0], left[0], left[1]], axis=0), jnp.concatenate([high, low_part, high], axis=0), ((0,), (0,))
    )
    for b in range(2):
        for k in range(8):
            gram[b, k] = share[64 * b + 8 * k:64 * b + 8 * k + 8]
    gram_x[me8] = gram[y % 2, me8]
    for i in (2, 1, 3, 0):
        for k in range(2):
            if i or k:
                xp, cp = (x + i) % NX, (c + k) % 2
                remote(gram.at[y % 2, 2 * xp + cp], gram_x.at[me8], gxs, gxr, dev(xp, y, z, cp)).start()
    for p in range(EARLY, NZ // 2):
        send_columns(p)

    remote(yg.at[pl.ds(0, 3)], yg.at[pl.ds(0, 3)], ags, agr, partner).wait_recv()
    for i in range(NX):
        yt[:, i * ROWS:(i + 1) * ROWS] = yg[i].T
    remote(peak_z.at[pl.ds(0, 7)], peak_z.at[pl.ds(0, 7)], pzs, pzr, partner).wait_recv()
    peak = peak_among(peak_z)[:, :1] * 1024.0

    fth[...], ftl[...] = split(yt[...] * (1.0 / peak))
    swaps = [None] * NZ

    def form(p):
        slots = (2 * p, 2 * p + 1)
        got_columns(p).wait_recv()
        cols = split(jnp.concatenate([xg[:, s].reshape(NX * ROWS, CHUNK) for s in slots], axis=1))
        value = dot3((fth[...], ftl[...]), cols)
        for i, s in enumerate(slots):
            for h in range(2):
                lp[s, h] = value[h * HALF:(h + 1) * HALF, i * CHUNK:(i + 1) * CHUNK]
            swaps[s] = remote(lp.at[s, other], lp_peer.at[s], ps.at[s], pr.at[s], partner)
            swaps[s].start()

    def held(s):
        swaps[s].wait_recv()
        return (lp[s, c] + lp_peer[s]).reshape(SUBS, SUB, CHUNK)

    ups = [[remote(up.at[s, q], up_in.at[s, q], us.at[s, q], ur.at[s, q], above) for q in range(SUBS)] for s in range(4)]
    downs = [
        [remote(down.at[s, q], down_in.at[s, q], ds.at[s, q], dr.at[s, q], below) for q in range(SUBS)] for s in range(3)
    ]

    def hop(s):
        ahead = held(2 * s)
        back = held(2 * s + 1) if s < 3 else None
        for q in range(SUBS):
            value = ahead[q]
            if s:
                ups[s - 1][q].wait_recv()
                value = value + up_in[s - 1, q]
            up[s, q] = value
            ups[s][q].start()
            if s == 3:
                continue
            value = back[q]
            if s:
                downs[s - 1][q].wait_recv()
                value = value + down_in[s - 1, q]
            down[s, q] = value
            downs[s][q].start()

    form(0)
    form(1)
    hop(0)

    remote(gram_x.at[pl.ds(0, 7)], gram_x.at[pl.ds(0, 7)], gxs, gxr, partner).wait_recv()
    total = gram_x[0]
    for k in range(1, 8):
        total = total + gram_x[k]
    gram_z[z] = total
    for i in (4, 3, 5, 2, 6, 1, 7):
        remote(gram_z.at[z], gram_z.at[z], gzs, gzr, dev(x, y, (z + i) % NZ, c)).start()

    form(2)
    hop(1)

    remote(gram_z.at[pl.ds(0, 7)], gram_z.at[pl.ds(0, 7)], gzs, gzr, partner).wait_recv()
    total = gram_z[0]
    for k in range(1, NZ):
        total = total + gram_z[k]
    block = 8 * y + me8
    corr[block] = total
    for i in (2, 1, 3, 0):
        for j in (2, 1, 3, 0):
            for k in range(2):
                if i or j or k:
                    to = dev((x + i) % NX, (y + j) % NY, z, (c + k) % 2)
                    remote(corr.at[block], corr.at[block], cs, cr, to).start()

    form(3)
    hop(2)
    hop(3)

    remote(corr.at[pl.ds(0, 31)], corr.at[pl.ds(0, 31)], cs, cr, partner).wait_recv()
    row = lax.broadcasted_iota(jnp.int32, (RANK, RANK), 0)
    col = lax.broadcasted_iota(jnp.int32, (RANK, RANK), 1)
    whole = corr[...].reshape(RANK, RANK)
    energy = jnp.sum(jnp.sum(jnp.where(row == col, whole, 0.0), axis=0, keepdims=True), axis=1, keepdims=True)
    scale = 1.0 / jnp.sqrt(energy)
    a1 = whole * scale * scale
    a1s = split(a1)
    a2 = dot3(a1s, a1s)
    a4 = dot3(split(a2), split(a2 - 9.0 * a1))
    poly = jnp.where(row == col, 2.25, 0.0) + (a4 + (27.0 * a2 - 39.0 * a1)) * 0.0625
    high, low_part = split(poly)
    for h in range(2):
        polh[h] = high[:, h * HALF:(h + 1) * HALF]
        poll[h] = low_part[:, h * HALF:(h + 1) * HALF]

    last = held(NZ - 1)
    for q in range(SUBS):
        downs[2][q].wait_recv()
        ups[3][q].wait_recv()
        full[c, q * SUB:(q + 1) * SUB] = (last[q] + down_in[2, q] + up_in[3, q]) * (peak * scale)
    share_full = remote(full.at[c], full.at[c], fs, fr, partner)
    share_full.start()
    value = dot3((polh[c], poll[c]), split(full[c]))
    share_full.wait_recv()
    value = value + dot3((polh[other], poll[other]), split(full[other]))
    value = jnp.where(c == 0, value, pltpu.roll(value, RANK - 4, 0))
    for k in range(NX * NZ):
        mixed[k] = value[8 * k:8 * k + 4]
    spot = NZ * x + z
    land[spot] = mixed[spot]
    for i in (2, 1, 3, 0):
        for j in (4, 3, 5, 2, 6, 1, 7, 0):
            if i or j:
                xp, zp = (x + i) % NX, (z + j) % NZ
                remote(mixed.at[NZ * xp + zp], land.at[spot], ms, mr, dev(xp, y, zp, c)).start()
    time_out[...] = dot3(split(yg[x] * scale), (high, low_part)) * math.sqrt(TIME)
    remote(land.at[pl.ds(0, 31)], land.at[pl.ds(0, 31)], ms, mr, partner).wait_recv()
    for k in range(NX * NZ):
        load_out[:, k * CHUNK:(k + 1) * CHUNK] = land[k]

    for copy in swaps + sum(ups + downs, []) + [share_full] + [got_columns(p) for p in range(NZ // 2)]:
        copy.wait_send()
    remote(py.at[pl.ds(0, 3)], py.at[pl.ds(0, 3)], ys, yr, partner).wait_send()
    remote(yg.at[pl.ds(0, 3)], yg.at[pl.ds(0, 3)], ags, agr, partner).wait_send()
    remote(gram_x.at[pl.ds(0, 7)], gram_x.at[pl.ds(0, 7)], gxs, gxr, partner).wait_send()
    remote(gram_z.at[pl.ds(0, 7)], gram_z.at[pl.ds(0, 7)], gzs, gzr, partner).wait_send()
    remote(corr.at[pl.ds(0, 31)], corr.at[pl.ds(0, 31)], cs, cr, partner).wait_send()
    remote(land.at[pl.ds(0, 31)], land.at[pl.ds(0, 31)], ms, mr, partner).wait_send()
    remote(peak_x.at[pl.ds(0, 7)], peak_x.at[pl.ds(0, 7)], pxs, pxr, partner).wait_send()
    remote(peak_y.at[pl.ds(0, 3)], peak_y.at[pl.ds(0, 3)], pys, pyr, partner).wait_send()
    remote(peak_z.at[pl.ds(0, 7)], peak_z.at[pl.ds(0, 7)], pzs, pzr, partner).wait_send()


def put_out(time, load, time_hbm, load_hbm, time_sem, load_sem):
    copies = [pltpu.make_async_copy(time, time_hbm, time_sem), pltpu.make_async_copy(load, load_hbm, load_sem)]
    for copy in copies:
        copy.start()
    for copy in copies:
        copy.wait()


def on_device(snapshots, space_factor):
    vm, dma = pltpu.VMEM, pltpu.SemaphoreType.DMA
    time, load = pl.pallas_call(
        kernel,
        name="hooi_time",
        out_shape=(vm((ROWS, RANK), F32), vm((RANK // 64, COLS), F32)),
        in_specs=[pl.BlockSpec(memory_space=pl.ANY)] * 2,
        out_specs=(pl.BlockSpec(memory_space=pltpu.VMEM),) * 2,
        scratch_shapes=[
            vm((ROWS, COLS), F32), vm((COLS, RANK), F32), vm((NY, ROWS, RANK), F32),
            vm((NX, ROWS, RANK), F32), vm((RANK, NX * ROWS), F32),
            vm((NX, NZ, ROWS, CHUNK), F32), vm((NX, NZ, ROWS, CHUNK), F32),
            vm((2, 8, 8, RANK), F32), vm((8, 8, RANK), F32), vm((NZ, 8, RANK), F32),
            vm((32, 8, RANK), F32),
            vm((RANK, RANK), BF16), vm((RANK, RANK), BF16),
            vm((2, RANK, HALF), BF16), vm((2, RANK, HALF), BF16),
            vm((NZ, 2, HALF, CHUNK), F32), vm((NZ, HALF, CHUNK), F32),
            vm((4, SUBS, SUB, CHUNK), F32), vm((4, SUBS, SUB, CHUNK), F32),
            vm((3, SUBS, SUB, CHUNK), F32), vm((3, SUBS, SUB, CHUNK), F32),
            vm((2, HALF, CHUNK), F32),
            vm((32, 4, CHUNK), F32), vm((32, 4, CHUNK), F32),
            vm((8, 1, 128), F32), vm((NY, 1, 128), F32), vm((NZ, 1, 128), F32),
            dma, dma((LOADS,)), dma((4,)), dma((4,)), dma, dma, dma, dma, dma, dma, dma, dma, dma, dma,
            dma((NZ,)), dma((NZ,)), dma((4, SUBS)), dma((4, SUBS)), dma((3, SUBS)), dma((3, SUBS)), dma, dma, dma, dma,
            dma, dma, dma, dma, dma, dma, pltpu.SemaphoreType.REGULAR((3,)),
        ],
        compiler_params=pltpu.CompilerParams(collective_id=0, has_side_effects=True),
    )(snapshots, space_factor)
    return pl.pallas_call(
        put_out,
        name="put_out",
        out_shape=(jax.ShapeDtypeStruct(time.shape, F32), jax.ShapeDtypeStruct(load.shape, F32)),
        in_specs=[pl.BlockSpec(memory_space=pltpu.VMEM)] * 2,
        out_specs=(pl.BlockSpec(memory_space=pl.ANY),) * 2,
        scratch_shapes=[dma, dma],
    )(pltpu.with_memory_space_constraint(time, pltpu.VMEM), pltpu.with_memory_space_constraint(load, pltpu.VMEM))


def solution(mesh):
    return jax.shard_map(
        on_device,
        mesh=mesh,
        in_specs=(P("tm", "space"), P("space", None)),
        out_specs=(P("tm", None), P("tm", "space")),
        check_vma=False,
    )
```

```python
import math

import jax
import jax.numpy as jnp
from jax import lax
from jax.experimental import pallas as pl
from jax.experimental.pallas import tpu as pltpu
from jax.sharding import PartitionSpec as P

MESH = pl.DeviceIdType.MESH
F32, BF16 = jnp.float32, jnp.bfloat16
RANK = 256
TIME = 4096
NX, NY, NZ = 4, 4, 8
ROWS = 64
COLS = 4096
WIDE = COLS // NX
CHUNK = WIDE // NZ
HALF = RANK // 2
LOADS = 8
EARLY = 2
SUBS = 2
SUB = HALF // SUBS


def split(value):
    high = value.astype(BF16)
    return high, (value - high.astype(F32)).astype(BF16)


def dot(left, right, dims=((1,), (0,))):
    return lax.dot_general(left, right, (dims, ((), ())), preferred_element_type=F32)


def dot3(left, right, dims=((1,), (0,))):
    return dot(left[0], right[0], dims) + (dot(left[0], right[1], dims) + dot(left[1], right[0], dims))


def kernel(
    snap_hbm, space_hbm, time_out, load_out,
    xv, sv, py, yg, yt, xc, xg, gram, gram_x, gram_z, corr, fth, ftl, polh, poll,
    lp, lp_peer, up, up_in, down, down_in, full, mixed, peak_x, peak_y, peak_z,
    ld_x, ld_s, xs, xr, ys, yr, ags, agr, gxs, gxr, gzs, gzr, cs, cr, ps, pr,
    us, ur, ds, dr, fs, fr, ms, mr, pxs, pxr, pys, pyr, pzs, pzr, near,
):
    t, y = lax.axis_index("tm"), lax.axis_index("space")
    x, z, c = t // 16, (t // 2) % NZ, t % 2
    other = 1 - c

    def dev(x_, y_, z_, c_):
        return {"tm": x_ * 16 + z_ * 2 + c_, "space": y_}

    def remote(src, dst, send, recv, to):
        return pltpu.make_async_remote_copy(
            src_ref=src, dst_ref=dst, send_sem=send, recv_sem=recv, device_id=to, device_id_type=MESH
        )

    partner = dev(x, y, z, other)
    above, below = dev(x, y, (z + 1) % NZ, c), dev(x, y, (z + 7) % NZ, c)
    me8 = 2 * x + c

    def peak_of(value):
        value = jnp.max(jnp.max(value, axis=0, keepdims=True), axis=1, keepdims=True)
        return jnp.broadcast_to(value, (1, 128))

    def peak_among(ref):
        value = ref[0]
        for k in range(1, ref.shape[0]):
            value = jnp.maximum(value, ref[k])
        return value

    depth = COLS // LOADS
    loads = []
    for i in range(LOADS):
        piece = pl.ds(i * depth, depth)
        loads.append(pltpu.make_async_copy(snap_hbm.at[:, piece], xv.at[:, piece], ld_x.at[i]))
        loads.append(pltpu.make_async_copy(space_hbm.at[piece], sv.at[piece], ld_s.at[i]))
    for copy in loads:
        copy.start()

    barrier = pltpu.get_barrier_semaphore()
    greeted = [partner, above, below] + [dev(x, (y + i) % NY, z, c) for i in (2, 1, 3)]
    greeted += [dev((x + i) % NX, y, z, k) for i in (2, 1, 3) for k in range(2)]
    for to in greeted:
        pl.semaphore_signal(barrier, inc=1, device_id=to, device_id_type=MESH)

    acc = jnp.zeros((ROWS, RANK), F32)
    acc2 = jnp.zeros((2 * ROWS, RANK), F32)
    for i in range(LOADS):
        loads[2 * i].wait()
        loads[2 * i + 1].wait()
        xh, xl = split(xv[:, i * depth:(i + 1) * depth])
        sh, sl = split(sv[i * depth:(i + 1) * depth, :])
        acc2 = acc2 + dot(jnp.concatenate([xh, xl], axis=0), sh)
        acc = acc + dot(xh, sl)
    py[y] = acc2[:ROWS] + (acc2[ROWS:] + acc)
    pl.semaphore_wait(barrier, len(greeted))

    for i in (2, 1, 3):
        remote(py.at[y], py.at[y], ys, yr, dev(x, (y + i) % NY, z, c)).start()

    def pass_on(step):
        for to in (above, below):
            pl.semaphore_signal(near.at[step], inc=1, device_id=to, device_id_type=MESH)

    pass_on(0)
    peak_x[me8] = peak_of(jnp.abs(py[y]))
    for i in (2, 1, 3, 0):
        for k in range(2):
            if i or k:
                remote(peak_x.at[me8], peak_x.at[me8], pxs, pxr, dev((x + i) % NX, y, z, (c + k) % 2)).start()

    order = [(z + 4) % NZ, (z + 5) % NZ, (z + 3) % NZ, (z + 6) % NZ, (z + 2) % NZ, (z + 7) % NZ, (z + 1) % NZ, z]
    for s in range(NZ):
        for i in range(NX):
            xc[i, s] = xv[:, pl.ds(pl.multiple_of(i * WIDE + order[s] * CHUNK, CHUNK), CHUNK)]

    def send_columns(p):
        slots = pl.ds(2 * p, 2)
        for i in (2, 1, 3):
            xp = (x + i) % NX
            remote(xc.at[xp, slots], xg.at[x, slots], xs.at[p], xr.at[p], dev(xp, y, z, c)).start()

    def got_columns(p):
        some = xg.at[pl.ds(0, 3), pl.ds(2 * p, 2)]
        return remote(some, some, xs.at[p], xr.at[p], partner)

    for p in range(EARLY):
        send_columns(p)
    xg[x] = xc[x]
    pl.semaphore_wait(near.at[0], 2)
    pass_on(1)
    remote(peak_x.at[pl.ds(0, 7)], peak_x.at[pl.ds(0, 7)], pxs, pxr, partner).wait_recv()
    peak_y[y] = peak_among(peak_x)
    for i in (2, 1, 3):
        remote(peak_y.at[y], peak_y.at[y], pys, pyr, dev(x, (y + i) % NY, z, c)).start()
    pl.semaphore_wait(near.at[1], 2)
    pass_on(2)
    remote(py.at[pl.ds(0, 3)], py.at[pl.ds(0, 3)], ys, yr, partner).wait_recv()
    mine = (py[0] + py[1]) + (py[2] + py[3])

    yg[x] = mine

    left = split(yg[x, :, pl.ds(pl.multiple_of(y // 2 * HALF, HALF), HALF)])
    high, low_part = split(mine)
    share = dot(
        jnp.concatenate([left[0], left[0], left[1]], axis=0), jnp.concatenate([high, low_part, high], axis=0), ((0,), (0,))
    )
    for b in range(2):
        for k in range(8):
            gram[b, k] = share[64 * b + 8 * k:64 * b + 8 * k + 8]
    gram_x[me8] = gram[y % 2, me8]
    for i in (2, 1, 3, 0):
        for k in range(2):
            if i or k:
                xp, cp = (x + i) % NX, (c + k) % 2
                remote(gram.at[y % 2, 2 * xp + cp], gram_x.at[me8], gxs, gxr, dev(xp, y, z, cp)).start()
    for i in (2, 1, 3):
        remote(yg.at[x], yg.at[x], ags, agr, dev((x + i) % NX, y, z, c)).start()

    remote(peak_y.at[pl.ds(0, 3)], peak_y.at[pl.ds(0, 3)], pys, pyr, partner).wait_recv()
    peak_z[z] = peak_among(peak_y)
    pl.semaphore_wait(near.at[2], 2)
    for i in (4, 3, 5, 2, 6, 1, 7):
        remote(peak_z.at[z], peak_z.at[z], pzs, pzr, dev(x, y, (z + i) % NZ, c)).start()

    for p in range(EARLY, NZ // 2):
        send_columns(p)

    remote(yg.at[pl.ds(0, 3)], yg.at[pl.ds(0, 3)], ags, agr, partner).wait_recv()
    for i in range(NX):
        yt[:, i * ROWS:(i + 1) * ROWS] = yg[i].T
    remote(peak_z.at[pl.ds(0, 7)], peak_z.at[pl.ds(0, 7)], pzs, pzr, partner).wait_recv()
    peak = peak_among(peak_z)[:, :1] * 1024.0

    fth[...], ftl[...] = split(yt[...] * (1.0 / peak))
    swaps = [None] * NZ

    def form(p):
        slots = (2 * p, 2 * p + 1)
        got_columns(p).wait_recv()
        cols = split(jnp.concatenate([xg[:, s].reshape(NX * ROWS, CHUNK) for s in slots], axis=1))
        value = dot3((fth[...], ftl[...]), cols)
        for i, s in enumerate(slots):
            for h in range(2):
                lp[s, h] = value[h * HALF:(h + 1) * HALF, i * CHUNK:(i + 1) * CHUNK]
            swaps[s] = remote(lp.at[s, other], lp_peer.at[s], ps.at[s], pr.at[s], partner)
            swaps[s].start()

    def held(s):
        swaps[s].wait_recv()
        return (lp[s, c] + lp_peer[s]).reshape(SUBS, SUB, CHUNK)

    up_to = [above, dev(x, y, (z + 2) % NZ, c), above, above]
    ups = [
        [remote(up.at[s, q], up_in.at[s, q], us.at[s, q], ur.at[s, q], up_to[s]) for q in range(SUBS)] for s in range(4)
    ]
    downs = [
        [remote(down.at[s, q], down_in.at[s, q], ds.at[s, q], dr.at[s, q], below) for q in range(SUBS)] for s in range(3)
    ]

    def send_up(s, slot, joins):
        block = held(slot)
        for q in range(SUBS):
            value = block[q]
            for k in joins:
                ups[k][q].wait_recv()
                value = value + up_in[k, q]
            up[s, q] = value
            ups[s][q].start()

    def send_down(s, slot, joins):
        block = held(slot)
        for q in range(SUBS):
            value = block[q]
            for k in joins:
                downs[k][q].wait_recv()
                value = value + down_in[k, q]
            down[s, q] = value
            downs[s][q].start()

    form(0)
    form(1)

    remote(gram_x.at[pl.ds(0, 7)], gram_x.at[pl.ds(0, 7)], gxs, gxr, partner).wait_recv()
    total = gram_x[0]
    for k in range(1, 8):
        total = total + gram_x[k]
    gram_z[z] = total
    for i in (4, 3, 5, 2, 6, 1, 7):
        remote(gram_z.at[z], gram_z.at[z], gzs, gzr, dev(x, y, (z + i) % NZ, c)).start()

    send_up(0, 0, ())
    send_down(0, 1, ())

    form(2)
    send_up(1, 2, (0,))

    remote(gram_z.at[pl.ds(0, 7)], gram_z.at[pl.ds(0, 7)], gzs, gzr, partner).wait_recv()
    total = gram_z[0]
    for k in range(1, NZ):
        total = total + gram_z[k]
    block = 8 * y + me8
    corr[block] = total
    for i in (2, 1, 3, 0):
        for j in (2, 1, 3, 0):
            for k in range(2):
                if i or j or k:
                    to = dev((x + i) % NX, (y + j) % NY, z, (c + k) % 2)
                    remote(corr.at[block], corr.at[block], cs, cr, to).start()

    send_down(1, 3, (0,))
    send_up(2, 4, ())

    form(3)
    send_down(2, 5, (1,))
    send_up(3, 6, (2, 1))

    remote(corr.at[pl.ds(0, 31)], corr.at[pl.ds(0, 31)], cs, cr, partner).wait_recv()
    row = lax.broadcasted_iota(jnp.int32, (RANK, RANK), 0)
    col = lax.broadcasted_iota(jnp.int32, (RANK, RANK), 1)
    whole = corr[...].reshape(RANK, RANK)
    energy = jnp.sum(jnp.sum(jnp.where(row == col, whole, 0.0), axis=0, keepdims=True), axis=1, keepdims=True)
    scale = 1.0 / jnp.sqrt(energy)
    a1 = whole * scale * scale
    a1s = split(a1)
    a2 = dot3(a1s, a1s)
    a4 = dot3(split(a2), split(a2 - 9.0 * a1))
    poly = jnp.where(row == col, 2.25, 0.0) + (a4 + (27.0 * a2 - 39.0 * a1)) * 0.0625
    high, low_part = split(poly)
    for h in range(2):
        polh[h] = high[:, h * HALF:(h + 1) * HALF]
        poll[h] = low_part[:, h * HALF:(h + 1) * HALF]

    last = held(NZ - 1)
    for q in range(SUBS):
        downs[2][q].wait_recv()
        ups[3][q].wait_recv()
        full[c, q * SUB:(q + 1) * SUB] = (last[q] + down_in[2, q] + up_in[3, q]) * (peak * scale)
    share_full = remote(full.at[c], full.at[c], fs, fr, partner)
    share_full.start()
    value = dot3((polh[c], poll[c]), split(full[c]))
    share_full.wait_recv()
    value = value + dot3((polh[other], poll[other]), split(full[other]))
    value = jnp.where(c == 0, value, pltpu.roll(value, RANK - 4, 0))
    for k in range(NX * NZ):
        mixed[k] = value[8 * k:8 * k + 4]
    spot = NZ * x + z
    here = pl.ds(pl.multiple_of(spot * CHUNK, CHUNK), CHUNK)
    load_out[:, here] = mixed[spot]
    for i in (2, 1, 3, 0):
        for j in (4, 3, 5, 2, 6, 1, 7, 0):
            if i or j:
                xp, zp = (x + i) % NX, (z + j) % NZ
                remote(mixed.at[NZ * xp + zp], load_out.at[:, here], ms, mr, dev(xp, y, zp, c)).start()
    time_out[...] = dot3(split(yg[x] * scale), (high, low_part)) * math.sqrt(TIME)
    remote(mixed.at[pl.ds(0, 31)], mixed.at[pl.ds(0, 31)], ms, mr, partner).wait_recv()

    for copy in swaps + sum(ups + downs, []) + [share_full] + [got_columns(p) for p in range(NZ // 2)]:
        copy.wait_send()
    remote(py.at[pl.ds(0, 3)], py.at[pl.ds(0, 3)], ys, yr, partner).wait_send()
    remote(yg.at[pl.ds(0, 3)], yg.at[pl.ds(0, 3)], ags, agr, partner).wait_send()
    remote(gram_x.at[pl.ds(0, 7)], gram_x.at[pl.ds(0, 7)], gxs, gxr, partner).wait_send()
    remote(gram_z.at[pl.ds(0, 7)], gram_z.at[pl.ds(0, 7)], gzs, gzr, partner).wait_send()
    remote(corr.at[pl.ds(0, 31)], corr.at[pl.ds(0, 31)], cs, cr, partner).wait_send()
    remote(mixed.at[pl.ds(0, 31)], mixed.at[pl.ds(0, 31)], ms, mr, partner).wait_send()
    remote(peak_x.at[pl.ds(0, 7)], peak_x.at[pl.ds(0, 7)], pxs, pxr, partner).wait_send()
    remote(peak_y.at[pl.ds(0, 3)], peak_y.at[pl.ds(0, 3)], pys, pyr, partner).wait_send()
    remote(peak_z.at[pl.ds(0, 7)], peak_z.at[pl.ds(0, 7)], pzs, pzr, partner).wait_send()


def put_out(time, load, time_hbm, load_hbm, time_sem, load_sem):
    copies = [pltpu.make_async_copy(time, time_hbm, time_sem), pltpu.make_async_copy(load, load_hbm, load_sem)]
    for copy in copies:
        copy.start()
    for copy in copies:
        copy.wait()


def on_device(snapshots, space_factor):
    vm, dma = pltpu.VMEM, pltpu.SemaphoreType.DMA
    time, load = pl.pallas_call(
        kernel,
        name="hooi_time",
        out_shape=(vm((ROWS, RANK), F32), vm((RANK // 64, COLS), F32)),
        in_specs=[pl.BlockSpec(memory_space=pl.ANY)] * 2,
        out_specs=(pl.BlockSpec(memory_space=pltpu.VMEM),) * 2,
        scratch_shapes=[
            vm((ROWS, COLS), F32), vm((COLS, RANK), F32), vm((NY, ROWS, RANK), F32),
            vm((NX, ROWS, RANK), F32), vm((RANK, NX * ROWS), F32),
            vm((NX, NZ, ROWS, CHUNK), F32), vm((NX, NZ, ROWS, CHUNK), F32),
            vm((2, 8, 8, RANK), F32), vm((8, 8, RANK), F32), vm((NZ, 8, RANK), F32),
            vm((32, 8, RANK), F32),
            vm((RANK, RANK), BF16), vm((RANK, RANK), BF16),
            vm((2, RANK, HALF), BF16), vm((2, RANK, HALF), BF16),
            vm((NZ, 2, HALF, CHUNK), F32), vm((NZ, HALF, CHUNK), F32),
            vm((4, SUBS, SUB, CHUNK), F32), vm((4, SUBS, SUB, CHUNK), F32),
            vm((3, SUBS, SUB, CHUNK), F32), vm((3, SUBS, SUB, CHUNK), F32),
            vm((2, HALF, CHUNK), F32),
            vm((32, 4, CHUNK), F32),
            vm((8, 1, 128), F32), vm((NY, 1, 128), F32), vm((NZ, 1, 128), F32),
            dma((LOADS,)), dma((LOADS,)), dma((4,)), dma((4,)), dma, dma, dma, dma, dma, dma, dma, dma, dma, dma,
            dma((NZ,)), dma((NZ,)), dma((4, SUBS)), dma((4, SUBS)), dma((3, SUBS)), dma((3, SUBS)), dma, dma, dma, dma,
            dma, dma, dma, dma, dma, dma, pltpu.SemaphoreType.REGULAR((3,)),
        ],
        compiler_params=pltpu.CompilerParams(collective_id=0, has_side_effects=True),
    )(snapshots, space_factor)
    return pl.pallas_call(
        put_out,
        name="put_out",
        out_shape=(jax.ShapeDtypeStruct(time.shape, F32), jax.ShapeDtypeStruct(load.shape, F32)),
        in_specs=[pl.BlockSpec(memory_space=pltpu.VMEM)] * 2,
        out_specs=(pl.BlockSpec(memory_space=pl.ANY),) * 2,
        scratch_shapes=[dma, dma],
    )(pltpu.with_memory_space_constraint(time, pltpu.VMEM), pltpu.with_memory_space_constraint(load, pltpu.VMEM))


def solution(mesh):
    return jax.shard_map(
        on_device,
        mesh=mesh,
        in_specs=(P("tm", "space"), P("space", None)),
        out_specs=(P("tm", None), P("tm", "space")),
        check_vma=False,
    )
```

```python
import math

import jax
import jax.numpy as jnp
from jax import lax
from jax.experimental import pallas as pl
from jax.experimental.pallas import tpu as pltpu
from jax.sharding import PartitionSpec as P

MESH = pl.DeviceIdType.MESH
F32, BF16 = jnp.float32, jnp.bfloat16
RANK = 256
TIME = 4096
NX, NY, NZ = 4, 4, 8
ROWS = 64
COLS = 4096
WIDE = COLS // NX
CHUNK = WIDE // NZ
HALF = RANK // 2
LOADS = 8
EARLY = 2
SUBS = 4
SUB = HALF // SUBS


def split(value):
    high = value.astype(BF16)
    return high, (value - high.astype(F32)).astype(BF16)


def dot(left, right, dims=((1,), (0,))):
    return lax.dot_general(left, right, (dims, ((), ())), preferred_element_type=F32)


def dot3(left, right, dims=((1,), (0,))):
    return dot(left[0], right[0], dims) + (dot(left[0], right[1], dims) + dot(left[1], right[0], dims))


def kernel(
    snap_hbm, space_hbm, time_out, load_out,
    xv, sv, py, yg, yt, xc, xg, gram, gram_x, gram_z, corr, fth, ftl, polh, poll,
    lp, lp_peer, up, up_in, down, down_in, full, mixed, peak_x, peak_y, peak_z,
    ld_x, ld_s, xs, xr, ys, yr, ags, agr, gxs, gxr, gzs, gzr, cs, cr, ps, pr,
    us, ur, ds, dr, fs, fr, ms, mr, pxs, pxr, pys, pyr, pzs, pzr, near,
):
    t, y = lax.axis_index("tm"), lax.axis_index("space")
    x, z, c = t // 16, (t // 2) % NZ, t % 2
    other = 1 - c

    def dev(x_, y_, z_, c_):
        return {"tm": x_ * 16 + z_ * 2 + c_, "space": y_}

    def remote(src, dst, send, recv, to):
        return pltpu.make_async_remote_copy(
            src_ref=src, dst_ref=dst, send_sem=send, recv_sem=recv, device_id=to, device_id_type=MESH
        )

    partner = dev(x, y, z, other)
    above, below = dev(x, y, (z + 1) % NZ, c), dev(x, y, (z + 7) % NZ, c)
    me8 = 2 * x + c

    def peak_of(value):
        value = jnp.max(jnp.max(value, axis=0, keepdims=True), axis=1, keepdims=True)
        return jnp.broadcast_to(value, (1, 128))

    def peak_among(ref):
        value = ref[0]
        for k in range(1, ref.shape[0]):
            value = jnp.maximum(value, ref[k])
        return value

    depth = COLS // LOADS
    loads = []
    for i in range(LOADS):
        piece = pl.ds(i * depth, depth)
        loads.append(pltpu.make_async_copy(snap_hbm.at[:, piece], xv.at[:, piece], ld_x.at[i]))
        loads.append(pltpu.make_async_copy(space_hbm.at[piece], sv.at[piece], ld_s.at[i]))
    for copy in loads:
        copy.start()

    barrier = pltpu.get_barrier_semaphore()
    greeted = [partner, above, below] + [dev(x, (y + i) % NY, z, c) for i in (2, 1, 3)]
    greeted += [dev((x + i) % NX, y, z, k) for i in (2, 1, 3) for k in range(2)]
    for to in greeted:
        pl.semaphore_signal(barrier, inc=1, device_id=to, device_id_type=MESH)

    acc = jnp.zeros((ROWS, RANK), F32)
    acc2 = jnp.zeros((2 * ROWS, RANK), F32)
    for i in range(LOADS):
        loads[2 * i].wait()
        loads[2 * i + 1].wait()
        xh, xl = split(xv[:, i * depth:(i + 1) * depth])
        sh, sl = split(sv[i * depth:(i + 1) * depth, :])
        acc2 = acc2 + dot(jnp.concatenate([xh, xl], axis=0), sh)
        acc = acc + dot(xh, sl)
    py[y] = acc2[:ROWS] + (acc2[ROWS:] + acc)
    pl.semaphore_wait(barrier, len(greeted))

    for i in (2, 1, 3):
        remote(py.at[y], py.at[y], ys, yr, dev(x, (y + i) % NY, z, c)).start()

    def pass_on(step):
        for to in (above, below):
            pl.semaphore_signal(near.at[step], inc=1, device_id=to, device_id_type=MESH)

    pass_on(0)
    peak_x[me8] = peak_of(jnp.abs(py[y]))
    for i in (2, 1, 3, 0):
        for k in range(2):
            if i or k:
                remote(peak_x.at[me8], peak_x.at[me8], pxs, pxr, dev((x + i) % NX, y, z, (c + k) % 2)).start()

    order = [(z + 4) % NZ, (z + 5) % NZ, (z + 3) % NZ, (z + 6) % NZ, (z + 2) % NZ, (z + 7) % NZ, (z + 1) % NZ, z]
    for s in range(NZ):
        for i in range(NX):
            xc[i, s] = xv[:, pl.ds(pl.multiple_of(i * WIDE + order[s] * CHUNK, CHUNK), CHUNK)]

    def send_columns(p):
        slots = pl.ds(2 * p, 2)
        for i in (2, 1, 3):
            xp = (x + i) % NX
            remote(xc.at[xp, slots], xg.at[x, slots], xs.at[p], xr.at[p], dev(xp, y, z, c)).start()

    def got_columns(p):
        some = xg.at[pl.ds(0, 3), pl.ds(2 * p, 2)]
        return remote(some, some, xs.at[p], xr.at[p], partner)

    for p in range(EARLY):
        send_columns(p)
    xg[x] = xc[x]
    pl.semaphore_wait(near.at[0], 2)
    pass_on(1)
    remote(peak_x.at[pl.ds(0, 7)], peak_x.at[pl.ds(0, 7)], pxs, pxr, partner).wait_recv()
    peak_y[y] = peak_among(peak_x)
    for i in (2, 1, 3):
        remote(peak_y.at[y], peak_y.at[y], pys, pyr, dev(x, (y + i) % NY, z, c)).start()
    pl.semaphore_wait(near.at[1], 2)
    pass_on(2)
    remote(py.at[pl.ds(0, 3)], py.at[pl.ds(0, 3)], ys, yr, partner).wait_recv()
    mine = (py[0] + py[1]) + (py[2] + py[3])

    yg[x] = mine

    for i in (2, 1, 3):
        remote(yg.at[x], yg.at[x], ags, agr, dev((x + i) % NX, y, z, c)).start()

    remote(peak_y.at[pl.ds(0, 3)], peak_y.at[pl.ds(0, 3)], pys, pyr, partner).wait_recv()
    peak_z[z] = peak_among(peak_y)
    pl.semaphore_wait(near.at[2], 2)
    for i in (4, 3, 5, 2, 6, 1, 7):
        remote(peak_z.at[z], peak_z.at[z], pzs, pzr, dev(x, y, (z + i) % NZ, c)).start()


    left = split(yg[x, :, pl.ds(pl.multiple_of(y // 2 * HALF, HALF), HALF)])
    high, low_part = split(mine)
    share = dot(
        jnp.concatenate([left[0], left[0], left[1]], axis=0), jnp.concatenate([high, low_part, high], axis=0), ((0,), (0,))
    )
    for b in range(2):
        for k in range(8):
            gram[b, k] = share[64 * b + 8 * k:64 * b + 8 * k + 8]
    gram_x[me8] = gram[y % 2, me8]
    for i in (2, 1, 3, 0):
        for k in range(2):
            if i or k:
                xp, cp = (x + i) % NX, (c + k) % 2
                remote(gram.at[y % 2, 2 * xp + cp], gram_x.at[me8], gxs, gxr, dev(xp, y, z, cp)).start()
    for p in range(EARLY, NZ // 2):
        send_columns(p)

    remote(yg.at[pl.ds(0, 3)], yg.at[pl.ds(0, 3)], ags, agr, partner).wait_recv()
    for i in range(NX):
        yt[:, i * ROWS:(i + 1) * ROWS] = yg[i].T
    remote(peak_z.at[pl.ds(0, 7)], peak_z.at[pl.ds(0, 7)], pzs, pzr, partner).wait_recv()
    peak = peak_among(peak_z)[:, :1] * 1024.0

    fth[...], ftl[...] = split(yt[...] * (1.0 / peak))
    swaps = [None] * NZ

    def form(p):
        slots = (2 * p, 2 * p + 1)
        got_columns(p).wait_recv()
        cols = split(jnp.concatenate([xg[:, s].reshape(NX * ROWS, CHUNK) for s in slots], axis=1))
        value = dot3((fth[...], ftl[...]), cols)
        for i, s in enumerate(slots):
            for h in range(2):
                lp[s, h] = value[h * HALF:(h + 1) * HALF, i * CHUNK:(i + 1) * CHUNK]
            swaps[s] = remote(lp.at[s, other], lp_peer.at[s], ps.at[s], pr.at[s], partner)
            swaps[s].start()

    def held(s):
        swaps[s].wait_recv()
        return (lp[s, c] + lp_peer[s]).reshape(SUBS, SUB, CHUNK)

    up_to = [above, dev(x, y, (z + 2) % NZ, c), above, above]
    ups = [
        [remote(up.at[s, q], up_in.at[s, q], us.at[s, q], ur.at[s, q], up_to[s]) for q in range(SUBS)] for s in range(4)
    ]
    downs = [
        [remote(down.at[s, q], down_in.at[s, q], ds.at[s, q], dr.at[s, q], below) for q in range(SUBS)] for s in range(3)
    ]

    def send_up(s, slot, joins):
        block = held(slot)
        for q in range(SUBS):
            value = block[q]
            for k in joins:
                ups[k][q].wait_recv()
                value = value + up_in[k, q]
            up[s, q] = value
            ups[s][q].start()

    def send_down(s, slot, joins):
        block = held(slot)
        for q in range(SUBS):
            value = block[q]
            for k in joins:
                downs[k][q].wait_recv()
                value = value + down_in[k, q]
            down[s, q] = value
            downs[s][q].start()

    form(0)
    form(1)

    remote(gram_x.at[pl.ds(0, 7)], gram_x.at[pl.ds(0, 7)], gxs, gxr, partner).wait_recv()
    total = gram_x[0]
    for k in range(1, 8):
        total = total + gram_x[k]
    gram_z[z] = total
    for i in (4, 3, 5, 2, 6, 1, 7):
        remote(gram_z.at[z], gram_z.at[z], gzs, gzr, dev(x, y, (z + i) % NZ, c)).start()

    send_up(0, 0, ())
    send_down(0, 1, ())

    form(2)
    send_up(1, 2, (0,))

    remote(gram_z.at[pl.ds(0, 7)], gram_z.at[pl.ds(0, 7)], gzs, gzr, partner).wait_recv()
    total = gram_z[0]
    for k in range(1, NZ):
        total = total + gram_z[k]
    block = 8 * y + me8
    corr[block] = total
    for i in (2, 1, 3, 0):
        for j in (2, 1, 3, 0):
            for k in range(2):
                if i or j or k:
                    to = dev((x + i) % NX, (y + j) % NY, z, (c + k) % 2)
                    remote(corr.at[block], corr.at[block], cs, cr, to).start()

    send_down(1, 3, (0,))
    send_up(2, 4, ())

    form(3)
    send_down(2, 5, (1,))
    send_up(3, 6, (2, 1))

    remote(corr.at[pl.ds(0, 31)], corr.at[pl.ds(0, 31)], cs, cr, partner).wait_recv()
    row = lax.broadcasted_iota(jnp.int32, (RANK, RANK), 0)
    col = lax.broadcasted_iota(jnp.int32, (RANK, RANK), 1)
    whole = corr[...].reshape(RANK, RANK)
    energy = jnp.sum(jnp.sum(jnp.where(row == col, whole, 0.0), axis=0, keepdims=True), axis=1, keepdims=True)
    scale = 1.0 / jnp.sqrt(energy)
    a1 = whole * scale * scale
    a1s = split(a1)
    a2 = dot3(a1s, a1s)
    a4 = dot3(split(a2), split(a2 - 9.0 * a1))
    poly = jnp.where(row == col, 2.25, 0.0) + (a4 + (27.0 * a2 - 39.0 * a1)) * 0.0625
    high, low_part = split(poly)
    for h in range(2):
        polh[h] = high[:, h * HALF:(h + 1) * HALF]
        poll[h] = low_part[:, h * HALF:(h + 1) * HALF]

    last = held(NZ - 1)
    for q in range(SUBS):
        downs[2][q].wait_recv()
        ups[3][q].wait_recv()
        full[c, q * SUB:(q + 1) * SUB] = (last[q] + down_in[2, q] + up_in[3, q]) * (peak * scale)
    share_full = remote(full.at[c], full.at[c], fs, fr, partner)
    share_full.start()
    value = dot3((polh[c], poll[c]), split(full[c]))
    share_full.wait_recv()
    value = value + dot3((polh[other], poll[other]), split(full[other]))
    value = jnp.where(c == 0, value, pltpu.roll(value, RANK - 4, 0))
    for k in range(NX * NZ):
        mixed[k] = value[8 * k:8 * k + 4]
    spot = NZ * x + z
    here = pl.ds(pl.multiple_of(spot * CHUNK, CHUNK), CHUNK)
    load_out[:, here] = mixed[spot]
    for i in (2, 1, 3, 0):
        for j in (4, 3, 5, 2, 6, 1, 7, 0):
            if i or j:
                xp, zp = (x + i) % NX, (z + j) % NZ
                remote(mixed.at[NZ * xp + zp], load_out.at[:, here], ms, mr, dev(xp, y, zp, c)).start()
    time_out[...] = dot3(split(yg[x] * scale), (high, low_part)) * math.sqrt(TIME)
    remote(mixed.at[pl.ds(0, 31)], mixed.at[pl.ds(0, 31)], ms, mr, partner).wait_recv()

    for copy in swaps + sum(ups + downs, []) + [share_full] + [got_columns(p) for p in range(NZ // 2)]:
        copy.wait_send()
    remote(py.at[pl.ds(0, 3)], py.at[pl.ds(0, 3)], ys, yr, partner).wait_send()
    remote(yg.at[pl.ds(0, 3)], yg.at[pl.ds(0, 3)], ags, agr, partner).wait_send()
    remote(gram_x.at[pl.ds(0, 7)], gram_x.at[pl.ds(0, 7)], gxs, gxr, partner).wait_send()
    remote(gram_z.at[pl.ds(0, 7)], gram_z.at[pl.ds(0, 7)], gzs, gzr, partner).wait_send()
    remote(corr.at[pl.ds(0, 31)], corr.at[pl.ds(0, 31)], cs, cr, partner).wait_send()
    remote(mixed.at[pl.ds(0, 31)], mixed.at[pl.ds(0, 31)], ms, mr, partner).wait_send()
    remote(peak_x.at[pl.ds(0, 7)], peak_x.at[pl.ds(0, 7)], pxs, pxr, partner).wait_send()
    remote(peak_y.at[pl.ds(0, 3)], peak_y.at[pl.ds(0, 3)], pys, pyr, partner).wait_send()
    remote(peak_z.at[pl.ds(0, 7)], peak_z.at[pl.ds(0, 7)], pzs, pzr, partner).wait_send()


def put_out(time, load, time_hbm, load_hbm, time_sem, load_sem):
    copies = [pltpu.make_async_copy(time, time_hbm, time_sem), pltpu.make_async_copy(load, load_hbm, load_sem)]
    for copy in copies:
        copy.start()
    for copy in copies:
        copy.wait()


def on_device(snapshots, space_factor):
    vm, dma = pltpu.VMEM, pltpu.SemaphoreType.DMA
    time, load = pl.pallas_call(
        kernel,
        name="hooi_time",
        out_shape=(vm((ROWS, RANK), F32), vm((RANK // 64, COLS), F32)),
        in_specs=[pl.BlockSpec(memory_space=pl.ANY)] * 2,
        out_specs=(pl.BlockSpec(memory_space=pltpu.VMEM),) * 2,
        scratch_shapes=[
            vm((ROWS, COLS), F32), vm((COLS, RANK), F32), vm((NY, ROWS, RANK), F32),
            vm((NX, ROWS, RANK), F32), vm((RANK, NX * ROWS), F32),
            vm((NX, NZ, ROWS, CHUNK), F32), vm((NX, NZ, ROWS, CHUNK), F32),
            vm((2, 8, 8, RANK), F32), vm((8, 8, RANK), F32), vm((NZ, 8, RANK), F32),
            vm((32, 8, RANK), F32),
            vm((RANK, RANK), BF16), vm((RANK, RANK), BF16),
            vm((2, RANK, HALF), BF16), vm((2, RANK, HALF), BF16),
            vm((NZ, 2, HALF, CHUNK), F32), vm((NZ, HALF, CHUNK), F32),
            vm((4, SUBS, SUB, CHUNK), F32), vm((4, SUBS, SUB, CHUNK), F32),
            vm((3, SUBS, SUB, CHUNK), F32), vm((3, SUBS, SUB, CHUNK), F32),
            vm((2, HALF, CHUNK), F32),
            vm((32, 4, CHUNK), F32),
            vm((8, 1, 128), F32), vm((NY, 1, 128), F32), vm((NZ, 1, 128), F32),
            dma((LOADS,)), dma((LOADS,)), dma((4,)), dma((4,)), dma, dma, dma, dma, dma, dma, dma, dma, dma, dma,
            dma((NZ,)), dma((NZ,)), dma((4, SUBS)), dma((4, SUBS)), dma((3, SUBS)), dma((3, SUBS)), dma, dma, dma, dma,
            dma, dma, dma, dma, dma, dma, pltpu.SemaphoreType.REGULAR((3,)),
        ],
        compiler_params=pltpu.CompilerParams(collective_id=0, has_side_effects=True),
    )(snapshots, space_factor)
    return pl.pallas_call(
        put_out,
        name="put_out",
        out_shape=(jax.ShapeDtypeStruct(time.shape, F32), jax.ShapeDtypeStruct(load.shape, F32)),
        in_specs=[pl.BlockSpec(memory_space=pltpu.VMEM)] * 2,
        out_specs=(pl.BlockSpec(memory_space=pl.ANY),) * 2,
        scratch_shapes=[dma, dma],
    )(pltpu.with_memory_space_constraint(time, pltpu.VMEM), pltpu.with_memory_space_constraint(load, pltpu.VMEM))


def solution(mesh):
    return jax.shard_map(
        on_device,
        mesh=mesh,
        in_specs=(P("tm", "space"), P("space", None)),
        out_specs=(P("tm", None), P("tm", "space")),
        check_vma=False,
    )
```

```python
import math

import jax
import jax.numpy as jnp
from jax import lax
from jax.experimental import pallas as pl
from jax.experimental.pallas import tpu as pltpu
from jax.sharding import PartitionSpec as P

MESH = pl.DeviceIdType.MESH
F32, BF16 = jnp.float32, jnp.bfloat16
RANK = 256
TIME = 4096
NX, NY, NZ = 4, 4, 8
ROWS = 64
COLS = 4096
WIDE = COLS // NX
CHUNK = WIDE // NZ
HALF = RANK // 2
LOADS = 8
EARLY = 2
SUBS = 4
SUB = HALF // SUBS


def split(value):
    high = value.astype(BF16)
    return high, (value - high.astype(F32)).astype(BF16)


def dot(left, right, dims=((1,), (0,))):
    return lax.dot_general(left, right, (dims, ((), ())), preferred_element_type=F32)


def dot3(left, right, dims=((1,), (0,))):
    return dot(left[0], right[0], dims) + (dot(left[0], right[1], dims) + dot(left[1], right[0], dims))


def kernel(
    snap_hbm, space_hbm, time_out, load_out,
    xv, sv, py, yg, yt, xc, xg, gram, gram_x, gram_z, corr, fth, ftl, polh, poll,
    lp, lp_peer, up, up_in, down, down_in, full, mixed, peak_x, peak_y, peak_z,
    ld_x, ld_s, xs, xr, ys, yr, ags, agr, gxs, gxr, gzs, gzr, cs, cr, ps, pr,
    us, ur, ds, dr, fs, fr, ms, mr, pxs, pxr, pys, pyr, pzs, pzr, near,
):
    t, y = lax.axis_index("tm"), lax.axis_index("space")
    x, z, c = t // 16, (t // 2) % NZ, t % 2
    other = 1 - c

    def dev(x_, y_, z_, c_):
        return {"tm": x_ * 16 + z_ * 2 + c_, "space": y_}

    def remote(src, dst, send, recv, to):
        return pltpu.make_async_remote_copy(
            src_ref=src, dst_ref=dst, send_sem=send, recv_sem=recv, device_id=to, device_id_type=MESH
        )

    partner = dev(x, y, z, other)
    above, below = dev(x, y, (z + 1) % NZ, c), dev(x, y, (z + 7) % NZ, c)
    me8 = 2 * x + c

    def peak_of(value):
        value = jnp.max(jnp.max(value, axis=0, keepdims=True), axis=1, keepdims=True)
        return jnp.broadcast_to(value, (1, 128))

    def peak_among(ref):
        value = ref[0]
        for k in range(1, ref.shape[0]):
            value = jnp.maximum(value, ref[k])
        return value

    depth = COLS // LOADS
    loads = []
    for i in range(LOADS):
        piece = pl.ds(i * depth, depth)
        loads.append(pltpu.make_async_copy(snap_hbm.at[:, piece], xv.at[:, piece], ld_x.at[i]))
        loads.append(pltpu.make_async_copy(space_hbm.at[piece], sv.at[piece], ld_s.at[i]))
    for copy in loads:
        copy.start()

    barrier = pltpu.get_barrier_semaphore()
    greeted = [partner, above, below] + [dev(x, (y + i) % NY, z, c) for i in (2, 1, 3)]
    greeted += [dev((x + i) % NX, y, z, k) for i in (2, 1, 3) for k in range(2)]
    for to in greeted:
        pl.semaphore_signal(barrier, inc=1, device_id=to, device_id_type=MESH)

    acc = jnp.zeros((ROWS, RANK), F32)
    acc2 = jnp.zeros((2 * ROWS, RANK), F32)
    for i in range(LOADS):
        loads[2 * i].wait()
        loads[2 * i + 1].wait()
        xh, xl = split(xv[:, i * depth:(i + 1) * depth])
        sh, sl = split(sv[i * depth:(i + 1) * depth, :])
        acc2 = acc2 + dot(jnp.concatenate([xh, xl], axis=0), sh)
        acc = acc + dot(xh, sl)
    py[y] = acc2[:ROWS] + (acc2[ROWS:] + acc)
    pl.semaphore_wait(barrier, len(greeted))

    for i in (2, 1, 3):
        remote(py.at[y], py.at[y], ys, yr, dev(x, (y + i) % NY, z, c)).start()

    def pass_on(step):
        for to in (above, below):
            pl.semaphore_signal(near.at[step], inc=1, device_id=to, device_id_type=MESH)

    pass_on(0)
    peak_x[me8] = peak_of(jnp.abs(py[y]))
    for i in (2, 1, 3, 0):
        for k in range(2):
            if i or k:
                remote(peak_x.at[me8], peak_x.at[me8], pxs, pxr, dev((x + i) % NX, y, z, (c + k) % 2)).start()

    order = [(z + 4) % NZ, (z + 5) % NZ, (z + 3) % NZ, (z + 6) % NZ, (z + 2) % NZ, (z + 7) % NZ, (z + 1) % NZ, z]
    for s in range(NZ):
        for i in range(NX):
            xc[i, s] = xv[:, pl.ds(pl.multiple_of(i * WIDE + order[s] * CHUNK, CHUNK), CHUNK)]

    def send_columns(p):
        slots = pl.ds(2 * p, 2)
        for i in (2, 1, 3):
            xp = (x + i) % NX
            remote(xc.at[xp, slots], xg.at[x, slots], xs.at[p], xr.at[p], dev(xp, y, z, c)).start()

    def got_columns(p):
        some = xg.at[pl.ds(0, 3), pl.ds(2 * p, 2)]
        return remote(some, some, xs.at[p], xr.at[p], partner)

    for p in range(EARLY):
        send_columns(p)
    xg[x] = xc[x]
    pl.semaphore_wait(near.at[0], 2)
    pass_on(1)
    remote(peak_x.at[pl.ds(0, 7)], peak_x.at[pl.ds(0, 7)], pxs, pxr, partner).wait_recv()
    peak_y[y] = peak_among(peak_x)
    for i in (2, 1, 3):
        remote(peak_y.at[y], peak_y.at[y], pys, pyr, dev(x, (y + i) % NY, z, c)).start()
    pl.semaphore_wait(near.at[1], 2)
    pass_on(2)
    remote(py.at[pl.ds(0, 3)], py.at[pl.ds(0, 3)], ys, yr, partner).wait_recv()
    mine = (py[0] + py[1]) + (py[2] + py[3])

    yg[x] = mine

    for i in (2, 1, 3):
        remote(yg.at[x], yg.at[x], ags, agr, dev((x + i) % NX, y, z, c)).start()

    remote(peak_y.at[pl.ds(0, 3)], peak_y.at[pl.ds(0, 3)], pys, pyr, partner).wait_recv()
    peak_z[z] = peak_among(peak_y)
    pl.semaphore_wait(near.at[2], 2)
    for i in (4, 3, 5, 2, 6, 1, 7):
        remote(peak_z.at[z], peak_z.at[z], pzs, pzr, dev(x, y, (z + i) % NZ, c)).start()


    left = split(yg[x, :, pl.ds(pl.multiple_of(y // 2 * HALF, HALF), HALF)])
    high, low_part = split(mine)
    share = dot(
        jnp.concatenate([left[0], left[0], left[1]], axis=0), jnp.concatenate([high, low_part, high], axis=0), ((0,), (0,))
    )
    for b in range(2):
        for k in range(8):
            gram[b, k] = share[64 * b + 8 * k:64 * b + 8 * k + 8]
    gram_x[me8] = gram[y % 2, me8]
    for i in (2, 1, 3, 0):
        for k in range(2):
            if i or k:
                xp, cp = (x + i) % NX, (c + k) % 2
                remote(gram.at[y % 2, 2 * xp + cp], gram_x.at[me8], gxs, gxr, dev(xp, y, z, cp)).start()
    send_columns(2)

    remote(yg.at[pl.ds(0, 3)], yg.at[pl.ds(0, 3)], ags, agr, partner).wait_recv()
    for i in range(NX):
        yt[:, i * ROWS:(i + 1) * ROWS] = yg[i].T
    remote(peak_z.at[pl.ds(0, 7)], peak_z.at[pl.ds(0, 7)], pzs, pzr, partner).wait_recv()
    peak = peak_among(peak_z)[:, :1] * 1024.0

    fth[...], ftl[...] = split(yt[...] * (1.0 / peak))
    swaps = [None] * NZ

    def form(p):
        slots = (2 * p, 2 * p + 1)
        got_columns(p).wait_recv()
        cols = split(jnp.concatenate([xg[:, s].reshape(NX * ROWS, CHUNK) for s in slots], axis=1))
        value = dot3((fth[...], ftl[...]), cols)
        for i, s in enumerate(slots):
            for h in range(2):
                lp[s, h] = value[h * HALF:(h + 1) * HALF, i * CHUNK:(i + 1) * CHUNK]
            swaps[s] = remote(lp.at[s, other], lp_peer.at[s], ps.at[s], pr.at[s], partner)
            swaps[s].start()

    def held(s):
        swaps[s].wait_recv()
        return (lp[s, c] + lp_peer[s]).reshape(SUBS, SUB, CHUNK)

    up_to = [above, dev(x, y, (z + 2) % NZ, c), above, above]
    ups = [
        [remote(up.at[s, q], up_in.at[s, q], us.at[s, q], ur.at[s, q], up_to[s]) for q in range(SUBS)] for s in range(4)
    ]
    downs = [
        [remote(down.at[s, q], down_in.at[s, q], ds.at[s, q], dr.at[s, q], below) for q in range(SUBS)] for s in range(3)
    ]

    def send_up(s, slot, joins):
        block = held(slot)
        for q in range(SUBS):
            value = block[q]
            for k in joins:
                ups[k][q].wait_recv()
                value = value + up_in[k, q]
            up[s, q] = value
            ups[s][q].start()

    def send_down(s, slot, joins):
        block = held(slot)
        for q in range(SUBS):
            value = block[q]
            for k in joins:
                downs[k][q].wait_recv()
                value = value + down_in[k, q]
            down[s, q] = value
            downs[s][q].start()

    form(0)
    form(1)

    remote(gram_x.at[pl.ds(0, 7)], gram_x.at[pl.ds(0, 7)], gxs, gxr, partner).wait_recv()
    total = gram_x[0]
    for k in range(1, 8):
        total = total + gram_x[k]
    gram_z[z] = total
    for i in (4, 3, 5, 2, 6, 1, 7):
        remote(gram_z.at[z], gram_z.at[z], gzs, gzr, dev(x, y, (z + i) % NZ, c)).start()

    send_columns(3)
    send_up(0, 0, ())
    send_down(0, 1, ())

    form(2)
    send_up(1, 2, (0,))

    remote(gram_z.at[pl.ds(0, 7)], gram_z.at[pl.ds(0, 7)], gzs, gzr, partner).wait_recv()
    total = gram_z[0]
    for k in range(1, NZ):
        total = total + gram_z[k]
    block = 8 * y + me8
    corr[block] = total
    for i in (2, 1, 3, 0):
        for j in (2, 1, 3, 0):
            for k in range(2):
                if i or j or k:
                    to = dev((x + i) % NX, (y + j) % NY, z, (c + k) % 2)
                    remote(corr.at[block], corr.at[block], cs, cr, to).start()

    send_down(1, 3, (0,))
    send_up(2, 4, ())

    form(3)
    send_down(2, 5, (1,))
    send_up(3, 6, (2, 1))

    remote(corr.at[pl.ds(0, 31)], corr.at[pl.ds(0, 31)], cs, cr, partner).wait_recv()
    row = lax.broadcasted_iota(jnp.int32, (RANK, RANK), 0)
    col = lax.broadcasted_iota(jnp.int32, (RANK, RANK), 1)
    whole = corr[...].reshape(RANK, RANK)
    energy = jnp.sum(jnp.sum(jnp.where(row == col, whole, 0.0), axis=0, keepdims=True), axis=1, keepdims=True)
    scale = 1.0 / jnp.sqrt(energy)
    a1 = whole * scale * scale
    a1s = split(a1)
    a2 = dot3(a1s, a1s)
    a4 = dot3(split(a2), split(a2 - 9.0 * a1))
    poly = jnp.where(row == col, 2.25, 0.0) + (a4 + (27.0 * a2 - 39.0 * a1)) * 0.0625
    high, low_part = split(poly)
    for h in range(2):
        polh[h] = high[:, h * HALF:(h + 1) * HALF]
        poll[h] = low_part[:, h * HALF:(h + 1) * HALF]

    last = held(NZ - 1)
    for q in range(SUBS):
        downs[2][q].wait_recv()
        ups[3][q].wait_recv()
        full[c, q * SUB:(q + 1) * SUB] = (last[q] + down_in[2, q] + up_in[3, q]) * (peak * scale)
    share_full = remote(full.at[c], full.at[c], fs, fr, partner)
    share_full.start()
    value = dot3((polh[c], poll[c]), split(full[c]))
    share_full.wait_recv()
    value = value + dot3((polh[other], poll[other]), split(full[other]))
    value = jnp.where(c == 0, value, pltpu.roll(value, RANK - 4, 0))
    for k in range(NX * NZ):
        mixed[k] = value[8 * k:8 * k + 4]
    spot = NZ * x + z
    here = pl.ds(pl.multiple_of(spot * CHUNK, CHUNK), CHUNK)
    load_out[:, here] = mixed[spot]
    for i in (2, 1, 3, 0):
        for j in (4, 3, 5, 2, 6, 1, 7, 0):
            if i or j:
                xp, zp = (x + i) % NX, (z + j) % NZ
                remote(mixed.at[NZ * xp + zp], load_out.at[:, here], ms, mr, dev(xp, y, zp, c)).start()
    time_out[...] = dot3(split(yg[x] * scale), (high, low_part)) * math.sqrt(TIME)
    remote(mixed.at[pl.ds(0, 31)], mixed.at[pl.ds(0, 31)], ms, mr, partner).wait_recv()

    for copy in swaps + sum(ups + downs, []) + [share_full] + [got_columns(p) for p in range(NZ // 2)]:
        copy.wait_send()
    remote(py.at[pl.ds(0, 3)], py.at[pl.ds(0, 3)], ys, yr, partner).wait_send()
    remote(yg.at[pl.ds(0, 3)], yg.at[pl.ds(0, 3)], ags, agr, partner).wait_send()
    remote(gram_x.at[pl.ds(0, 7)], gram_x.at[pl.ds(0, 7)], gxs, gxr, partner).wait_send()
    remote(gram_z.at[pl.ds(0, 7)], gram_z.at[pl.ds(0, 7)], gzs, gzr, partner).wait_send()
    remote(corr.at[pl.ds(0, 31)], corr.at[pl.ds(0, 31)], cs, cr, partner).wait_send()
    remote(mixed.at[pl.ds(0, 31)], mixed.at[pl.ds(0, 31)], ms, mr, partner).wait_send()
    remote(peak_x.at[pl.ds(0, 7)], peak_x.at[pl.ds(0, 7)], pxs, pxr, partner).wait_send()
    remote(peak_y.at[pl.ds(0, 3)], peak_y.at[pl.ds(0, 3)], pys, pyr, partner).wait_send()
    remote(peak_z.at[pl.ds(0, 7)], peak_z.at[pl.ds(0, 7)], pzs, pzr, partner).wait_send()


def put_out(time, load, time_hbm, load_hbm, time_sem, load_sem):
    copies = [pltpu.make_async_copy(time, time_hbm, time_sem), pltpu.make_async_copy(load, load_hbm, load_sem)]
    for copy in copies:
        copy.start()
    for copy in copies:
        copy.wait()


def on_device(snapshots, space_factor):
    vm, dma = pltpu.VMEM, pltpu.SemaphoreType.DMA
    time, load = pl.pallas_call(
        kernel,
        name="hooi_time",
        out_shape=(vm((ROWS, RANK), F32), vm((RANK // 64, COLS), F32)),
        in_specs=[pl.BlockSpec(memory_space=pl.ANY)] * 2,
        out_specs=(pl.BlockSpec(memory_space=pltpu.VMEM),) * 2,
        scratch_shapes=[
            vm((ROWS, COLS), F32), vm((COLS, RANK), F32), vm((NY, ROWS, RANK), F32),
            vm((NX, ROWS, RANK), F32), vm((RANK, NX * ROWS), F32),
            vm((NX, NZ, ROWS, CHUNK), F32), vm((NX, NZ, ROWS, CHUNK), F32),
            vm((2, 8, 8, RANK), F32), vm((8, 8, RANK), F32), vm((NZ, 8, RANK), F32),
            vm((32, 8, RANK), F32),
            vm((RANK, RANK), BF16), vm((RANK, RANK), BF16),
            vm((2, RANK, HALF), BF16), vm((2, RANK, HALF), BF16),
            vm((NZ, 2, HALF, CHUNK), F32), vm((NZ, HALF, CHUNK), F32),
            vm((4, SUBS, SUB, CHUNK), F32), vm((4, SUBS, SUB, CHUNK), F32),
            vm((3, SUBS, SUB, CHUNK), F32), vm((3, SUBS, SUB, CHUNK), F32),
            vm((2, HALF, CHUNK), F32),
            vm((32, 4, CHUNK), F32),
            vm((8, 1, 128), F32), vm((NY, 1, 128), F32), vm((NZ, 1, 128), F32),
            dma((LOADS,)), dma((LOADS,)), dma((4,)), dma((4,)), dma, dma, dma, dma, dma, dma, dma, dma, dma, dma,
            dma((NZ,)), dma((NZ,)), dma((4, SUBS)), dma((4, SUBS)), dma((3, SUBS)), dma((3, SUBS)), dma, dma, dma, dma,
            dma, dma, dma, dma, dma, dma, pltpu.SemaphoreType.REGULAR((3,)),
        ],
        compiler_params=pltpu.CompilerParams(collective_id=0, has_side_effects=True),
    )(snapshots, space_factor)
    return pl.pallas_call(
        put_out,
        name="put_out",
        out_shape=(jax.ShapeDtypeStruct(time.shape, F32), jax.ShapeDtypeStruct(load.shape, F32)),
        in_specs=[pl.BlockSpec(memory_space=pltpu.VMEM)] * 2,
        out_specs=(pl.BlockSpec(memory_space=pl.ANY),) * 2,
        scratch_shapes=[dma, dma],
    )(pltpu.with_memory_space_constraint(time, pltpu.VMEM), pltpu.with_memory_space_constraint(load, pltpu.VMEM))


def solution(mesh):
    return jax.shard_map(
        on_device,
        mesh=mesh,
        in_specs=(P("tm", "space"), P("space", None)),
        out_specs=(P("tm", None), P("tm", "space")),
        check_vma=False,
    )
```
